128 devices in a mesh: prow: 16 (over x, z), pcol: 8 (over y, core).
Axes of the slice: x: 4, y: 4, z: 4, core: 2. Of those that a mesh axis runs over, the one named last changes fastest.
Arguments:
- rhs: float32 [31, 64, 2048], P(None, None, 'prow'), may hold values from -6 to 6
- factor: bfloat16 [98, 2048, 2048], P(None, 'prow', 'pcol'), may hold values from -0.03125 to 0.03125
- inverse: bfloat16 [31, 2048, 2048], P(None, 'pcol', 'prow')
- pattern: int32 [98], replicated, may hold values 0 or 1
Outputs:
- solution: float32 [31, 64, 2048], P(None, None, 'prow')
- forward_solution: float32 [31, 64, 2048], P(None, None, 'pcol')
The draws below stay inside these ranges and needn't reach their ends.
All inputs are finite; a program needn't handle non-finite values.
Results may differ from the reference program's by a relative error of at most 0.011.
Values sent between devices are 32-bit elements; how exact they have to be, the bound alone decides.
No kernel may reach another device: no remote copies, remote signals or barrier semaphores. Data moves between devices by JAX's collectives and lax.ppermute only.
A program may use at most 64 MiB of HBM per device.

```python
import math
import jax
import jax.numpy as jnp
from jax import lax

W = 2048
R = 64
LEV = 5
NS = 31
NBLK = 98


def draw_inverse(key, part):
    first_key, second_key = jax.random.split(key)
    row_ids = lax.broadcasted_iota(jnp.int32, (NS, W, W), 1)
    col_ids = lax.broadcasted_iota(jnp.int32, (NS, W, W), 2)
    diagonal = jax.random.uniform(first_key, (NS, W, 1), jnp.float32, 1.0, 2.0)
    spread_part = jax.random.normal(second_key, (NS, W, W), jnp.float32) * 0.4 / math.sqrt(W)
    return jnp.where(row_ids == col_ids, diagonal, spread_part).astype(jnp.bfloat16)


def touch_ends(drawn, rng, low, largest):
    place = [jax.random.randint(jax.random.fold_in(rng, axis), (), 0, length) for axis, length in enumerate(drawn.shape)]
    widest = drawn.shape.index(max(drawn.shape))
    neighbour = place[:widest] + [(place[widest] + 1) % drawn.shape[widest]] + place[widest + 1:]
    return drawn.at[tuple(place)].set(low).at[tuple(neighbour)].set(largest)


def shard_levels(own_key, dims, cuts, low, largest):
    def one(axis_at, shards_of):
        heights = jax.random.uniform(jax.random.fold_in(jax.random.fold_in(own_key, 6), axis_at), (shards_of,), jnp.float32, low / len(cuts), largest / len(cuts))
        return jnp.repeat(jnp.exp(heights), dims[axis_at] // shards_of).reshape((-1,) + (1,) * (len(dims) - axis_at - 1))

    gain = one(*cuts[0])
    for cut in cuts[1:]:
        gain = gain * one(*cut)
    return gain


def scatter_about(own_key, dims, spread, reach, pieces=(), kind=jnp.bfloat16):
    gain = shard_levels(own_key, dims, pieces, -0.22, 0.18) if pieces else 1.0
    values = jax.random.normal(own_key, dims, jnp.float32) * spread * gain
    return jnp.minimum(jnp.maximum(values, -reach), reach).astype(kind)


def setup_inputs(seed: int = 0) -> dict:
    streams_of = jax.random.split(jax.random.key(seed), 5)
    return {
        "rhs": scatter_about(streams_of[0], (NS, R, W), 1.0, 6.0, ((2, 16),), jnp.float32),
        "factor": scatter_about(streams_of[1], (NBLK, W, W), (16 * W) ** -0.5, 0.03125, ((1, 16), (2, 8))),
        "inverse": draw_inverse(jax.random.fold_in(streams_of[4], 71), 0),
        "pattern": touch_ends((jax.random.randint(streams_of[3], (NBLK,), 0, 3) < 2).astype(jnp.int32), jax.random.fold_in(streams_of[3], 1), 0, 1),
    }


def block_start(tree_depth):
    return (tree_depth - 2) * 2 ** tree_depth + 2


def product(left, right, form):
    return jnp.einsum(form, left.astype(jnp.float32), right.astype(jnp.float32))


def reference(rhs, factor, inverse, pattern):
    live = pattern.astype(jnp.float32)
    partial_value = jnp.zeros(rhs.shape, jnp.float32)
    forward_levels = [None] * LEV
    for tree_depth in range(LEV - 1, -1, -1):
        first = 2 ** tree_depth - 1
        count = 2 ** tree_depth
        residual = rhs[first:first + count] - partial_value[first:first + count]
        rounded = lax.optimization_barrier(residual.astype(jnp.bfloat16))
        forward = product(rounded, inverse[first:first + count], "nrc,nwc->nrw")
        forward_levels[tree_depth] = forward
        narrow = lax.optimization_barrier(forward.astype(jnp.bfloat16))
        if tree_depth > 0:
            start = block_start(tree_depth)
            weights = live[start:start + count * tree_depth].reshape(count, tree_depth)
            for upward in range(1, tree_depth + 1):
                blocks = factor[start + upward - 1:start + count * tree_depth:tree_depth]
                terms = product(narrow, blocks, "nrc,nwc->nrw") * weights[:, upward - 1][:, None, None]
                groups = count >> upward
                terms = terms.reshape((groups, 2 ** upward) + terms.shape[1:]).sum(axis=1)
                target = 2 ** (tree_depth - upward) - 1
                partial_value = partial_value.at[target:target + groups].add(terms)
    solved = [None] * LEV
    solved_narrow = [None] * LEV
    for tree_depth in range(LEV):
        first = 2 ** tree_depth - 1
        count = 2 ** tree_depth
        target_vec = forward_levels[tree_depth]
        if tree_depth > 0:
            start = block_start(tree_depth)
            weights = live[start:start + count * tree_depth].reshape(count, tree_depth)
            gathered = jnp.zeros(target_vec.shape, jnp.float32)
            for upward in range(1, tree_depth + 1):
                blocks = factor[start + upward - 1:start + count * tree_depth:tree_depth]
                above = jnp.repeat(solved_narrow[tree_depth - upward], 2 ** upward, axis=0)
                gathered = gathered + product(above, blocks, "nrw,nwc->nrc") * weights[:, upward - 1][:, None, None]
            target_vec = target_vec - gathered
        rounded = lax.optimization_barrier(target_vec.astype(jnp.bfloat16))
        solution = product(rounded, inverse[first:first + count], "nrw,nwc->nrc")
        solved[tree_depth] = solution
        solved_narrow[tree_depth] = lax.optimization_barrier(solution.astype(jnp.bfloat16))
    return (jnp.concatenate(solved, axis=0), jnp.concatenate(forward_levels, axis=0))
```

```python
import jax
import jax.numpy as jnp
from jax import lax
from jax.sharding import PartitionSpec as P

LEV = 5
ROWS = 16
RING = [[0, 2, 4, 6], [1, 3, 5, 7]]
TWIN = [(i, i ^ 1) for i in range(8)]


def block_start(tree_depth):
    return (tree_depth - 2) * 2**tree_depth + 2


def one_shot_ring(values):
    copies = jnp.broadcast_to(values[None], (4,) + values.shape)
    parts = lax.all_to_all(copies, "pcol", 0, 0, axis_index_groups=RING)
    return parts.sum(axis=0)


def sum_columns(values):
    shape = values.shape
    flat = values.reshape(shape[0] * shape[1], shape[2])
    if shape[0] <= 2:
        flat = flat + lax.ppermute(flat, "pcol", TWIN)
        return lax.optimization_barrier(one_shot_ring(flat).reshape(shape))
    halves = flat.reshape(2, -1, shape[2])
    core = lax.axis_index("pcol") % 2
    mine = lax.dynamic_index_in_dim(halves, core, 0, keepdims=False)
    other = lax.dynamic_index_in_dim(halves, 1 - core, 0, keepdims=False)
    mine = mine + lax.ppermute(other, "pcol", TWIN)
    mine = one_shot_ring(mine)
    other = lax.ppermute(mine, "pcol", TWIN)
    both = jnp.where(core == 0, jnp.stack([mine, other]), jnp.stack([other, mine]))
    return lax.optimization_barrier(both.reshape(shape))


def sum_rows(values):
    shape = values.shape
    if shape[0] == 1:
        chunks = values.reshape(8, 8, 2, 128).transpose(0, 2, 1, 3).reshape(ROWS, 8, 128)
    else:
        chunks = values.reshape(ROWS, -1, shape[2])
    part = lax.all_to_all(chunks, "prow", 0, 0).sum(axis=0)
    copies = jnp.broadcast_to(part[None], chunks.shape)
    whole = lax.all_to_all(copies, "prow", 0, 0)
    if shape[0] == 1:
        whole = whole.reshape(8, 2, 8, 128).transpose(0, 2, 1, 3)
    return lax.optimization_barrier(whole.reshape(shape))


def per_device(rhs, factor, inverse, pattern):
    live = pattern.astype(jnp.float32)
    partial_value = jnp.zeros(rhs.shape, jnp.float32)
    forward_levels = [None] * LEV
    for tree_depth in range(LEV - 1, -1, -1):
        first = 2**tree_depth - 1
        count = 2**tree_depth
        residual = rhs[first : first + count]
        if tree_depth < LEV - 1:
            residual = residual - sum_columns(partial_value[first : first + count])
        rounded = residual.astype(jnp.bfloat16)
        pieces = jnp.einsum(
            "nrc,nwc->nrw",
            rounded,
            inverse[first : first + count],
            preferred_element_type=jnp.float32,
        )
        forward = sum_rows(pieces)
        forward_levels[tree_depth] = forward
        narrow = forward.astype(jnp.bfloat16)
        if tree_depth > 0:
            start = block_start(tree_depth)
            weights = live[start : start + count * tree_depth].reshape(count, tree_depth)
            for upward in range(1, tree_depth + 1):
                blocks = factor[start + upward - 1 : start + count * tree_depth : tree_depth]
                terms = jnp.einsum(
                    "nrc,nwc->nrw", narrow, blocks, preferred_element_type=jnp.float32
                )
                terms = terms * weights[:, upward - 1][:, None, None]
                groups = count >> upward
                terms = terms.reshape((groups, 2**upward) + terms.shape[1:]).sum(axis=1)
                target = 2 ** (tree_depth - upward) - 1
                partial_value = partial_value.at[target : target + groups].add(terms)
    solved = [None] * LEV
    solved_narrow = [None] * LEV
    for tree_depth in range(LEV):
        first = 2**tree_depth - 1
        count = 2**tree_depth
        target_vec = forward_levels[tree_depth]
        if tree_depth > 0:
            start = block_start(tree_depth)
            weights = live[start : start + count * tree_depth].reshape(count, tree_depth)
            gathered = jnp.zeros(target_vec.shape, jnp.float32)
            for upward in range(1, tree_depth + 1):
                blocks = factor[start + upward - 1 : start + count * tree_depth : tree_depth]
                above = jnp.repeat(solved_narrow[tree_depth - upward], 2**upward, axis=0)
                terms = jnp.einsum(
                    "nrw,nwc->nrc", above, blocks, preferred_element_type=jnp.float32
                )
                gathered = gathered + terms * weights[:, upward - 1][:, None, None]
            target_vec = target_vec - sum_rows(gathered)
        rounded = target_vec.astype(jnp.bfloat16)
        pieces = jnp.einsum(
            "nrw,nwc->nrc",
            rounded,
            inverse[first : first + count],
            preferred_element_type=jnp.float32,
        )
        solution = sum_columns(pieces)
        solved[tree_depth] = solution
        solved_narrow[tree_depth] = solution.astype(jnp.bfloat16)
    return (jnp.concatenate(solved, axis=0), jnp.concatenate(forward_levels, axis=0))


def solution(mesh):
    in_specs = (P(None, None, "prow"), P(None, "prow", "pcol"), P(None, "pcol", "prow"), P())
    out_specs = (P(None, None, "prow"), P(None, None, "pcol"))
    return jax.shard_map(
        per_device, mesh=mesh, in_specs=in_specs, out_specs=out_specs, check_vma=False
    )
```

```python
import jax
import jax.numpy as jnp
from jax import lax
from jax.sharding import PartitionSpec as P

LEV = 5
ROWS = 16
RING = [[0, 2, 4, 6], [1, 3, 5, 7]]
TWIN = [(i, i ^ 1) for i in range(8)]


def block_start(tree_depth):
    return (tree_depth - 2) * 2**tree_depth + 2


def blocks_of(array, tree_depth, upward):
    start = block_start(tree_depth)
    count = 2**tree_depth
    return array[start + upward - 1 : start + count * tree_depth : tree_depth]


def product(left, right, form):
    return jnp.einsum(form, left, right, preferred_element_type=jnp.float32)


def one_shot_ring(values):
    copies = jnp.broadcast_to(values[None], (4,) + values.shape)
    parts = lax.all_to_all(copies, "pcol", 0, 0, axis_index_groups=RING)
    return parts.sum(axis=0)


def sum_columns(values):
    shape = values.shape
    flat = values.reshape(-1, shape[-1])
    if flat.shape[0] <= 128:
        flat = flat + lax.ppermute(flat, "pcol", TWIN)
        return one_shot_ring(flat).reshape(shape)
    halves = flat.reshape(2, -1, shape[-1])
    core = lax.axis_index("pcol") % 2
    mine = lax.dynamic_index_in_dim(halves, core, 0, keepdims=False)
    other = lax.dynamic_index_in_dim(halves, 1 - core, 0, keepdims=False)
    mine = mine + lax.ppermute(other, "pcol", TWIN)
    mine = one_shot_ring(mine)
    other = lax.ppermute(mine, "pcol", TWIN)
    both = jnp.where(core == 0, jnp.stack([mine, other]), jnp.stack([other, mine]))
    return both.reshape(shape)


def sum_rows(values):
    shape = values.shape
    chunks = values.reshape(ROWS, -1, shape[-1])
    part = lax.all_to_all(chunks, "prow", 0, 0).sum(axis=0)
    copies = jnp.broadcast_to(part[None], chunks.shape)
    whole = lax.all_to_all(copies, "prow", 0, 0)
    return whole.reshape(shape)


def per_device(rhs, factor, inverse, pattern):
    live = pattern.astype(jnp.float32)
    bf16 = jnp.bfloat16
    halves = factor[0:2].reshape(2, 128, 2, 128).transpose(0, 2, 1, 3).reshape(2, 256, 128)
    top = jnp.concatenate([inverse[0:1], halves]).astype(jnp.float32)
    scale = jnp.concatenate([jnp.ones((1,), jnp.float32), live[0:2]])
    top = (lax.all_gather(top, "prow") * scale[:, None, None]).astype(bf16)
    inverse_top = top[:, 0]
    factor_top = top[:, 1:].reshape(ROWS, 2, 2, 128, 128)

    partial_value = [[] for _ in range(LEV)]
    forward_levels = [None] * LEV

    def push_up(narrow, tree_depth):
        count = 2**tree_depth
        for upward in range(1, tree_depth + 1):
            terms = product(narrow, blocks_of(factor, tree_depth, upward), "nrc,nwc->nrw")
            terms = terms * blocks_of(live, tree_depth, upward)[:, None, None]
            groups = count >> upward
            terms = terms.reshape((groups, 2**upward) + terms.shape[1:]).sum(axis=1)
            partial_value[tree_depth - upward].append(terms)

    for tree_depth in range(LEV - 1, 0, -1):
        first = 2**tree_depth - 1
        count = 2**tree_depth
        residual = rhs[first : first + count]
        if tree_depth < LEV - 1:
            residual = residual - sum_columns(sum(partial_value[tree_depth]))
        pieces = product(residual.astype(bf16), inverse[first : first + count], "nrc,nwc->nrw")
        if tree_depth > 1:
            forward_levels[tree_depth] = sum_rows(pieces)
            push_up(forward_levels[tree_depth].astype(bf16), tree_depth)

    here = (lax.axis_index("pcol") == 0).astype(jnp.float32)
    root_part = sum(partial_value[0])[0] - rhs[0] * here
    sent = jnp.concatenate([pieces[0], pieces[1], root_part], axis=1).reshape(ROWS, 4, 640)
    got = lax.all_to_all(sent, "prow", 0, 0)
    forward_1 = got[:, :, :512].sum(axis=0)
    root_part = got[:, :, 512:]
    for child in range(2):
        narrow = forward_1[:, 256 * child : 256 * child + 256].astype(bf16).reshape(4, 2, 128)
        root_part = root_part + product(narrow, factor_top[:, child], "rhc,phwc->prw")
    residual = -sum_columns(root_part)
    forward_0 = product(residual.astype(bf16), inverse_top, "prc,pwc->prw").sum(axis=0)
    solution_0 = sum_columns(product(forward_0.astype(bf16), inverse_top, "rw,pwc->prc"))
    narrow = solution_0.astype(bf16)
    target_1 = [
        forward_1[:, 256 * child : 256 * child + 256]
        - product(narrow, factor_top[:, child], "prw,phwc->prhc").sum(axis=0).reshape(4, 256)
        for child in range(2)
    ]
    same = jnp.concatenate(target_1 + [forward_1, forward_0], axis=1)
    sent = jnp.concatenate([jnp.broadcast_to(same[None], (ROWS, 4, 1280)), solution_0], axis=2)
    got = lax.all_to_all(sent, "prow", 0, 0).reshape(64, 1408)
    target_1 = jnp.stack([got[:, 0:256], got[:, 256:512]])
    forward_levels[1] = jnp.stack([got[:, 512:768], got[:, 768:1024]])
    forward_levels[0] = got[None, :, 1024:1280]

    gathered = [[] for _ in range(LEV)]

    def push_down(narrow, tree_depth):
        for lower in range(max(tree_depth + 1, 2), LEV):
            upward = lower - tree_depth
            above = jnp.repeat(narrow, 2**upward, axis=0)
            terms = product(above, blocks_of(factor, lower, upward), "nrw,nwc->nrc")
            gathered[lower].append(terms * blocks_of(live, lower, upward)[:, None, None])

    solved = [got[None, :, 1280:1408]] + [None] * (LEV - 1)
    push_down(solved[0].astype(bf16), 0)
    for tree_depth in range(1, LEV):
        first = 2**tree_depth - 1
        count = 2**tree_depth
        if tree_depth == 1:
            target_vec = target_1
        else:
            target_vec = forward_levels[tree_depth] - sum_rows(sum(gathered[tree_depth]))
        pieces = product(target_vec.astype(bf16), inverse[first : first + count], "nrw,nwc->nrc")
        solved[tree_depth] = sum_columns(pieces)
        push_down(solved[tree_depth].astype(bf16), tree_depth)
    return (jnp.concatenate(solved, axis=0), jnp.concatenate(forward_levels, axis=0))


def solution(mesh):
    in_specs = (P(None, None, "prow"), P(None, "prow", "pcol"), P(None, "pcol", "prow"), P())
    out_specs = (P(None, None, "prow"), P(None, None, "pcol"))
    return jax.shard_map(
        per_device, mesh=mesh, in_specs=in_specs, out_specs=out_specs, check_vma=False
    )
```

```python
import jax
import jax.numpy as jnp
from jax import lax
from jax.sharding import PartitionSpec as P

LEV = 5
ROWS = 16
RING = [[0, 2, 4, 6], [1, 3, 5, 7]]
RIGHT = [(i, (i + 2) % 8) for i in range(8)]
ACROSS = [(i, (i + 4) % 8) for i in range(8)]
LEFT = [(i, (i + 6) % 8) for i in range(8)]
TWIN = [(i, i ^ 1) for i in range(8)]


def block_start(tree_depth):
    return (tree_depth - 2) * 2**tree_depth + 2


def blocks_of(array, tree_depth, upward):
    start = block_start(tree_depth)
    count = 2**tree_depth
    return array[start + upward - 1 : start + count * tree_depth : tree_depth]


def product(left, right, form):
    return jnp.einsum(form, left, right, preferred_element_type=jnp.float32)


def one_shot_ring(values):
    if values.size <= 32768:
        across = lax.ppermute(values, "pcol", ACROSS)
        right = lax.ppermute(values, "pcol", RIGHT)
        left = lax.ppermute(values, "pcol", LEFT)
        return (values + across) + (left + right)
    copies = jnp.broadcast_to(values[None], (4,) + values.shape)
    parts = lax.all_to_all(copies, "pcol", 0, 0, axis_index_groups=RING)
    return parts.sum(axis=0)


def sum_columns(values):
    shape = values.shape
    flat = values.reshape(-1, shape[-1])
    if flat.shape[0] <= 128:
        flat = flat + lax.ppermute(flat, "pcol", TWIN)
        return one_shot_ring(flat).reshape(shape)
    halves = flat.reshape(2, -1, shape[-1])
    core = lax.axis_index("pcol") % 2
    mine = lax.dynamic_index_in_dim(halves, core, 0, keepdims=False)
    other = lax.dynamic_index_in_dim(halves, 1 - core, 0, keepdims=False)
    mine = mine + lax.ppermute(other, "pcol", TWIN)
    mine = one_shot_ring(mine)
    other = lax.ppermute(mine, "pcol", TWIN)
    both = jnp.where(core == 0, jnp.stack([mine, other]), jnp.stack([other, mine]))
    return both.reshape(shape)


def sum_rows(values):
    shape = values.shape
    chunks = values.reshape(ROWS, -1, shape[-1])
    part = lax.all_to_all(chunks, "prow", 0, 0).sum(axis=0)
    copies = jnp.broadcast_to(part[None], chunks.shape)
    whole = lax.all_to_all(copies, "prow", 0, 0)
    return whole.reshape(shape)


def gather_top(factor, inverse, live, after):
    halves = factor[0:2].reshape(2, 128, 2, 128).transpose(0, 2, 1, 3).reshape(2, 256, 128)
    top = jnp.concatenate([inverse[0:1], halves]).astype(jnp.float32)
    top, after = lax.optimization_barrier((top, after))
    scale = jnp.concatenate([jnp.ones((1,), jnp.float32), live[0:2]])
    top = (lax.all_gather(top, "prow") * scale[:, None, None]).astype(jnp.bfloat16)
    return top, after


def per_device(rhs, factor, inverse, pattern):
    live = pattern.astype(jnp.float32)
    bf16 = jnp.bfloat16
    partial_value = [[] for _ in range(LEV)]
    forward_levels = [None] * LEV

    def push_up(narrow, tree_depth):
        count = 2**tree_depth
        for upward in range(1, tree_depth + 1):
            terms = product(narrow, blocks_of(factor, tree_depth, upward), "nrc,nwc->nrw")
            terms = terms * blocks_of(live, tree_depth, upward)[:, None, None]
            groups = count >> upward
            terms = terms.reshape((groups, 2**upward) + terms.shape[1:]).sum(axis=1)
            partial_value[tree_depth - upward].append(terms)

    for tree_depth in range(LEV - 1, 0, -1):
        first = 2**tree_depth - 1
        count = 2**tree_depth
        residual = rhs[first : first + count]
        if tree_depth < LEV - 1:
            residual = residual - sum_columns(sum(partial_value[tree_depth]))
        if tree_depth == 1:
            residual, top = lax.optimization_barrier((residual, top))
        pieces = product(residual.astype(bf16), inverse[first : first + count], "nrc,nwc->nrw")
        if tree_depth > 1:
            forward = sum_rows(pieces)
            if tree_depth == LEV - 1:
                top, forward = gather_top(factor, inverse, live, forward)
            forward_levels[tree_depth] = forward
            push_up(forward_levels[tree_depth].astype(bf16), tree_depth)

    inverse_top = top[:, 0]
    factor_top = top[:, 1:].reshape(ROWS, 2, 2, 128, 128)
    here = (lax.axis_index("pcol") == 0).astype(jnp.float32)
    root_part = sum(partial_value[0])[0] - rhs[0] * here
    sent = jnp.concatenate([pieces[0], pieces[1], root_part], axis=1).reshape(ROWS, 4, 640)
    got = lax.all_to_all(sent, "prow", 0, 0)
    forward_1 = got[:, :, :512].sum(axis=0)
    root_part = got[:, :, 512:]
    for child in range(2):
        narrow = forward_1[:, 256 * child : 256 * child + 256].astype(bf16).reshape(4, 2, 128)
        root_part = root_part + product(narrow, factor_top[:, child], "rhc,phwc->prw")
    residual = -sum_columns(root_part)
    forward_0 = product(residual.astype(bf16), inverse_top, "prc,pwc->prw").sum(axis=0)
    solution_0 = sum_columns(product(forward_0.astype(bf16), inverse_top, "rw,pwc->prc"))
    narrow = solution_0.astype(bf16)
    target_1 = [
        forward_1[:, 256 * child : 256 * child + 256]
        - product(narrow, factor_top[:, child], "prw,phwc->prhc").sum(axis=0).reshape(4, 256)
        for child in range(2)
    ]
    same = jnp.concatenate(target_1 + [forward_1, forward_0], axis=1)
    sent = jnp.concatenate([jnp.broadcast_to(same[None], (ROWS, 4, 1280)), solution_0], axis=2)
    got = lax.all_to_all(sent, "prow", 0, 0).reshape(64, 1408)
    target_1 = jnp.stack([got[:, 0:256], got[:, 256:512]])
    forward_levels[1] = jnp.stack([got[:, 512:768], got[:, 768:1024]])
    forward_levels[0] = got[None, :, 1024:1280]

    gathered = [[] for _ in range(LEV)]

    def push_down(narrow, tree_depth):
        for lower in range(max(tree_depth + 1, 2), LEV):
            upward = lower - tree_depth
            above = jnp.repeat(narrow, 2**upward, axis=0)
            terms = product(above, blocks_of(factor, lower, upward), "nrw,nwc->nrc")
            gathered[lower].append(terms * blocks_of(live, lower, upward)[:, None, None])

    solved = [got[None, :, 1280:1408]] + [None] * (LEV - 1)
    push_down(solved[0].astype(bf16), 0)
    for tree_depth in range(1, LEV):
        first = 2**tree_depth - 1
        count = 2**tree_depth
        if tree_depth == 1:
            target_vec = target_1
        else:
            target_vec = forward_levels[tree_depth] - sum_rows(sum(gathered[tree_depth]))
        pieces = product(target_vec.astype(bf16), inverse[first : first + count], "nrw,nwc->nrc")
        solved[tree_depth] = sum_columns(pieces)
        push_down(solved[tree_depth].astype(bf16), tree_depth)
    return (jnp.concatenate(solved, axis=0), jnp.concatenate(forward_levels, axis=0))


def solution(mesh):
    in_specs = (P(None, None, "prow"), P(None, "prow", "pcol"), P(None, "pcol", "prow"), P())
    out_specs = (P(None, None, "prow"), P(None, None, "pcol"))
    return jax.shard_map(
        per_device, mesh=mesh, in_specs=in_specs, out_specs=out_specs, check_vma=False
    )
```

```python
import jax
import jax.numpy as jnp
from jax import lax
from jax.sharding import PartitionSpec as P

LEV = 5
ROWS = 16
TOP = 3
BACK = 3
TWIN = [(i, i ^ 1) for i in range(8)]
YRING = [[(i, (i + 2 * k) % 8) for i in range(8)] for k in (2, 1, 3)]
YGROUPS = [[0, 2, 4, 6], [1, 3, 5, 7]]
XRING = [[(i, (i + 4 * k) % 16) for i in range(16)] for k in (2, 1, 3)]
ZGROUPS = [[4 * x + z for z in range(4)] for x in range(4)]


def block_start(tree_depth):
    return (tree_depth - 2) * 2**tree_depth + 2


def blocks_of(array, tree_depth, upward):
    start = block_start(tree_depth)
    count = 2**tree_depth
    return array[start + upward - 1 : start + count * tree_depth : tree_depth]


def nodes_of(array, tree_depth):
    return array[2**tree_depth - 1 : 2 ** (tree_depth + 1) - 1]


def product(left, right, form):
    return jnp.einsum(form, left, right, preferred_element_type=jnp.float32)


def sum_ring(values, axis, ring):
    across, right, left = [lax.ppermute(values, axis, step) for step in ring]
    return (values + across) + (right + left)


def sum_y_ring(values):
    if values.size <= 32768:
        return sum_ring(values, "pcol", YRING)
    copies = jnp.broadcast_to(values[None], (4,) + values.shape)
    parts = lax.all_to_all(copies, "pcol", 0, 0, axis_index_groups=YGROUPS)
    return parts.sum(axis=0)


def sum_columns(values):
    shape = values.shape
    flat = values.reshape(-1, shape[-1])
    if flat.size <= 16384:
        flat = flat + lax.ppermute(flat, "pcol", TWIN)
        return sum_y_ring(flat).reshape(shape)
    halves = flat.reshape(2, -1, shape[-1])
    core = lax.axis_index("pcol") % 2
    mine = lax.dynamic_index_in_dim(halves, core, 0, keepdims=False)
    other = lax.dynamic_index_in_dim(halves, 1 - core, 0, keepdims=False)
    mine = mine + lax.ppermute(other, "pcol", TWIN)
    mine = sum_y_ring(mine)
    other = lax.ppermute(mine, "pcol", TWIN)
    both = jnp.where(core == 0, jnp.stack([mine, other]), jnp.stack([other, mine]))
    return both.reshape(shape)


def sum_x_ring(values):
    shape = values.shape
    return sum_ring(values.reshape(-1, shape[-1]), "prow", XRING).reshape(shape)


def scatter_rows(values):
    chunks = values.reshape(ROWS, -1, values.shape[-1])
    return lax.all_to_all(chunks, "prow", 0, 0).sum(axis=0)


def share_rows(part, shape):
    copies = jnp.broadcast_to(part[None], (ROWS,) + part.shape)
    return lax.all_to_all(copies, "prow", 0, 0).reshape(shape)


def sum_rows(values):
    return share_rows(scatter_rows(values), values.shape)


def gather_blocks(inverses, factors, weights, after):
    count = inverses.shape[0]
    halves = factors.reshape(-1, 128, 2, 128).transpose(0, 2, 1, 3).reshape(-1, 256, 128)
    own = jnp.concatenate([inverses, halves]).astype(jnp.float32)
    own, after = lax.optimization_barrier((own, after))
    scale = jnp.concatenate([jnp.ones((count,), jnp.float32), weights])
    whole = lax.all_gather(own, "prow", axis_index_groups=ZGROUPS)
    whole = (whole * scale[:, None, None]).astype(jnp.bfloat16)
    inverses = whole[:, :count].transpose(1, 2, 0, 3).reshape(count, 256, 512)
    factors = whole[:, count:].reshape(4, -1, 2, 128, 128)
    factors = factors.transpose(1, 0, 3, 2, 4).reshape(-1, 512, 256)
    return inverses, factors, after


def to_lanes(values):
    return jnp.concatenate([values[i] for i in range(values.shape[0])], axis=1)


def from_lanes(values, width):
    count = values.shape[1] // width
    return jnp.stack([values[:, width * i : width * i + width] for i in range(count)])


def per_device(rhs, factor, inverse, pattern):
    live = pattern.astype(jnp.float32)
    bf16 = jnp.bfloat16
    forward_levels = [None] * LEV
    partial_value = [[] for _ in range(LEV)]

    def push_up(narrow, tree_depth, factors, weights, values):
        count = 2**tree_depth
        for upward in range(1, tree_depth + 1):
            blocks = factors[upward - 1 :: tree_depth]
            terms = product(narrow, blocks, "nrc,nwc->nrw")
            if weights is not None:
                terms = terms * weights[upward - 1 :: tree_depth][:, None, None]
            groups = count >> upward
            terms = terms.reshape((groups, 2**upward) + terms.shape[1:]).sum(axis=1)
            values[tree_depth - upward].append(terms)

    def own_blocks(array, tree_depth):
        start = block_start(tree_depth)
        return array[start : start + 2**tree_depth * tree_depth]

    for tree_depth in range(LEV - 1, TOP - 2, -1):
        residual = nodes_of(rhs, tree_depth)
        if tree_depth < LEV - 1:
            residual = residual - sum_columns(sum(partial_value[tree_depth]))
        pieces = product(residual.astype(bf16), nodes_of(inverse, tree_depth), "nrc,nwc->nrw")
        if tree_depth < TOP:
            break
        part = scatter_rows(pieces)
        if tree_depth == LEV - 1:
            top_inverses, top_factors, part = gather_blocks(
                inverse[0:3], factor[0:10], live[0:10], part
            )
        forward = share_rows(part, pieces.shape)
        forward_levels[tree_depth] = forward
        push_up(
            forward.astype(bf16),
            tree_depth,
            own_blocks(factor, tree_depth),
            own_blocks(live, tree_depth),
            partial_value,
        )

    here = (lax.axis_index("pcol") == 0).astype(jnp.float32)
    sums = jnp.concatenate([sum(partial_value[1]), sum(partial_value[0])])
    order = jnp.concatenate([rhs[1:3], rhs[0:1]])
    sums = sums - order * here
    sent = jnp.concatenate([to_lanes(pieces), to_lanes(sums)], axis=1).reshape(4, 16, 1408)
    got = lax.all_to_all(sent, "prow", 0, 0, axis_index_groups=ZGROUPS)
    top_forward = [None] * LEV
    top_forward[2] = sum_x_ring(from_lanes(got[:, :, :1024].sum(axis=0), 256))
    sums = jnp.stack([to_lanes(got[:, :, 1024 + 128 * i : 1152 + 128 * i]) for i in range(3)])
    top_partial = [[sums[2:3]], [sums[0:2]]]
    inverse_at = {0: top_inverses[0:1], 1: top_inverses[1:3]}
    factor_at = {1: top_factors[0:2], 2: top_factors[2:10]}
    push_up(top_forward[2].astype(bf16), 2, factor_at[2], None, top_partial)
    for tree_depth in (1, 0):
        residual = -sum_columns(sum(top_partial[tree_depth]))
        pieces = product(residual.astype(bf16), inverse_at[tree_depth], "nrc,nwc->nrw")
        top_forward[tree_depth] = sum_x_ring(pieces)
        if tree_depth:
            push_up(top_forward[1].astype(bf16), 1, factor_at[1], None, top_partial)

    if BACK > 2:
        lower_inverses, lower_factors, ahead = gather_blocks(
            inverse[3:7], factor[10:34], live[10:34], top_forward[2]
        )
        inverse_at[2] = lower_inverses
        factor_at[3] = lower_factors
        chunk = lax.axis_index("prow") % 4
        own = forward_levels[3].reshape(8, 4, 16, 256)
        top_forward[3] = lax.dynamic_index_in_dim(own, chunk, 1, keepdims=False)

    top_solved = []
    for tree_depth in range(BACK + 1):
        target = top_forward[tree_depth]
        if tree_depth:
            terms = 0.0
            for upward in range(tree_depth, 0, -1):
                above = jnp.repeat(top_solved[tree_depth - upward], 2**upward, axis=0)
                blocks = factor_at[tree_depth][upward - 1 :: tree_depth]
                terms = terms + product(above, blocks, "nrw,nwc->nrc")
            target = target - sum_x_ring(terms)
        if tree_depth == BACK:
            break
        pieces = product(target.astype(bf16), inverse_at[tree_depth], "nrw,nwc->nrc")
        solution = sum_columns(pieces)
        top_solved.append(solution.astype(bf16))
        solved_here = solution if tree_depth == 0 else jnp.concatenate([solved_here, solution])

    same = to_lanes(jnp.concatenate([target] + top_forward[:TOP][::-1]))
    width = same.shape[1]
    apart = jnp.stack([to_lanes(solved_here[:, :, 128 * z : 128 * z + 128]) for z in range(4)])
    sent = jnp.concatenate([jnp.broadcast_to(same[None], (4, 16, width)), apart], axis=2)
    got = lax.all_to_all(sent, "prow", 0, 0, axis_index_groups=ZGROUPS).reshape(64, -1)
    target = from_lanes(got[:, : 256 * 2**BACK], 256)
    at = 256 * 2**BACK
    for tree_depth in range(TOP - 1, -1, -1):
        forward_levels[tree_depth] = from_lanes(got[:, at : at + 256 * 2**tree_depth], 256)
        at += 256 * 2**tree_depth
    solved_here = from_lanes(got[:, width:], 128)
    solved = [nodes_of(solved_here, tree_depth) for tree_depth in range(BACK)]
    solved += [None] * (LEV - BACK)

    gathered = [[] for _ in range(LEV)]

    def push_down(narrow, tree_depth):
        for lower in range(max(tree_depth + 1, BACK + 1), LEV):
            upward = lower - tree_depth
            above = jnp.repeat(narrow, 2**upward, axis=0)
            terms = product(above, blocks_of(factor, lower, upward), "nrw,nwc->nrc")
            gathered[lower].append(terms * blocks_of(live, lower, upward)[:, None, None])

    for tree_depth in range(BACK):
        push_down(solved[tree_depth].astype(bf16), tree_depth)
    for tree_depth in range(BACK, LEV):
        if tree_depth > BACK:
            target = forward_levels[tree_depth] - sum_rows(sum(gathered[tree_depth]))
        pieces = product(target.astype(bf16), nodes_of(inverse, tree_depth), "nrw,nwc->nrc")
        solved[tree_depth] = sum_columns(pieces)
        push_down(solved[tree_depth].astype(bf16), tree_depth)
    return (jnp.concatenate(solved, axis=0), jnp.concatenate(forward_levels, axis=0))


def solution(mesh):
    in_specs = (P(None, None, "prow"), P(None, "prow", "pcol"), P(None, "pcol", "prow"), P())
    out_specs = (P(None, None, "prow"), P(None, None, "pcol"))
    return jax.shard_map(
        per_device, mesh=mesh, in_specs=in_specs, out_specs=out_specs, check_vma=False
    )
```

```python
import jax
import jax.numpy as jnp
from jax import lax
from jax.experimental import pallas as pl
from jax.experimental.pallas import tpu as pltpu
from jax.sharding import PartitionSpec as P

LEV = 5
ROWS = 16
TOP = 3
TWIN = [(i, i ^ 1) for i in range(8)]
YRING = [[(i, (i + 2 * k) % 8) for i in range(8)] for k in (2, 1, 3)]
YGROUPS = [[0, 2, 4, 6], [1, 3, 5, 7]]
XRING = [[(i, (i + 4 * k) % 16) for i in range(16)] for k in (2, 1, 3)]
ZGROUPS = [[4 * x + z for z in range(4)] for x in range(4)]


def block_start(tree_depth):
    return (tree_depth - 2) * 2**tree_depth + 2


def blocks_of(array, tree_depth, upward):
    start = block_start(tree_depth)
    count = 2**tree_depth
    return array[start + upward - 1 : start + count * tree_depth : tree_depth]


def nodes_of(array, tree_depth):
    return array[2**tree_depth - 1 : 2 ** (tree_depth + 1) - 1]


def product(left, right, form):
    return jnp.einsum(form, left, right, preferred_element_type=jnp.float32)


def sum_ring(values, axis, ring):
    across, right, left = [lax.ppermute(values, axis, step) for step in ring]
    return (values + across) + (right + left)


def sum_y_ring(values):
    if values.size <= 32768:
        return sum_ring(values, "pcol", YRING)
    copies = jnp.broadcast_to(values[None], (4,) + values.shape)
    parts = lax.all_to_all(copies, "pcol", 0, 0, axis_index_groups=YGROUPS)
    return parts.sum(axis=0)


def sum_columns(values):
    shape = values.shape
    flat = values.reshape(-1, shape[-1])
    if flat.size <= 16384:
        flat = flat + lax.ppermute(flat, "pcol", TWIN)
        return sum_y_ring(flat).reshape(shape)
    halves = flat.reshape(2, -1, shape[-1])
    core = lax.axis_index("pcol") % 2
    mine = lax.dynamic_index_in_dim(halves, core, 0, keepdims=False)
    other = lax.dynamic_index_in_dim(halves, 1 - core, 0, keepdims=False)
    mine = mine + lax.ppermute(other, "pcol", TWIN)
    mine = sum_y_ring(mine)
    other = lax.ppermute(mine, "pcol", TWIN)
    both = jnp.where(core == 0, jnp.stack([mine, other]), jnp.stack([other, mine]))
    return both.reshape(shape)


def sum_x_ring(values):
    shape = values.shape
    return sum_ring(values.reshape(-1, shape[-1]), "prow", XRING).reshape(shape)


def scatter_rows(values):
    chunks = values.reshape(ROWS, -1, values.shape[-1])
    return lax.all_to_all(chunks, "prow", 0, 0).sum(axis=0)


def share_rows(part, shape):
    copies = jnp.broadcast_to(part[None], (ROWS,) + part.shape)
    return lax.all_to_all(copies, "prow", 0, 0).reshape(shape)


def sum_rows(values):
    return share_rows(scatter_rows(values), values.shape)


def round_inverses(whole, count):
    def kernel(blocks, out):
        for i in range(count):
            for z in range(4):
                out[i, :, 128 * z : 128 * z + 128] = blocks[z, i].astype(jnp.bfloat16)

    return pl.pallas_call(
        kernel,
        out_shape=jax.ShapeDtypeStruct((count, 256, 512), jnp.bfloat16),
        grid=(1,),
        in_specs=[pl.BlockSpec((4, count, 256, 128), lambda i: (0, 0, 0, 0))],
        out_specs=pl.BlockSpec((count, 256, 512), lambda i: (0, 0, 0)),
    )(whole)


def round_factors(whole, weights, first):
    count = whole.shape[1] - first

    def kernel(weights, blocks, out):
        weight = weights[pl.program_id(0)]
        for z in range(4):
            for h in range(2):
                values = blocks[z, 0, 128 * h : 128 * h + 128, :] * weight
                rows = slice(128 * z, 128 * z + 128)
                out[0, rows, 128 * h : 128 * h + 128] = values.astype(jnp.bfloat16)

    return pl.pallas_call(
        kernel,
        out_shape=jax.ShapeDtypeStruct((count, 512, 256), jnp.bfloat16),
        grid=(count,),
        in_specs=[
            pl.BlockSpec(memory_space=pltpu.SMEM),
            pl.BlockSpec((4, 1, 256, 128), lambda i: (0, i + first, 0, 0)),
        ],
        out_specs=pl.BlockSpec((1, 512, 256), lambda i: (i, 0, 0)),
    )(weights, whole)


def gather_blocks(inverses, factors, after):
    halves = factors.reshape(-1, 128, 2, 128).transpose(0, 2, 1, 3).reshape(-1, 256, 128)
    own = jnp.concatenate([inverses, halves]).astype(jnp.float32)
    own, after = lax.optimization_barrier((own, after))
    whole = lax.all_gather(own, "prow", axis_index_groups=ZGROUPS)
    return whole, after


def call(kernel, shapes, *operands):
    outs = [jax.ShapeDtypeStruct(shape, jnp.float32) for shape in shapes]
    return pl.pallas_call(kernel, out_shape=outs)(*operands)


def dot(left, right, contract):
    dims = (((1,), (contract,)), ((), ()))
    return lax.dot_general(left, right, dims, preferred_element_type=jnp.float32)


def enter_split(order, total, inverses, sums_1, sums_0, here):
    def kernel(here, order, total, inverses, sums_1, sums_0, out):
        for n in range(4):
            rounded = (order[3 + n] - total[n]).astype(jnp.bfloat16)
            piece = dot(rounded, inverses[n], 1)
            for z in range(4):
                out[z, :, 256 * n : 256 * n + 256] = piece[16 * z : 16 * z + 16]
        for i, value in enumerate((sums_1[0], sums_1[1], sums_0[0])):
            value = value - order[(i + 1) % 3] * here[0]
            for z in range(4):
                out[z, :, 1024 + 128 * i : 1152 + 128 * i] = value[16 * z : 16 * z + 16]

    specs = [pl.BlockSpec(memory_space=pltpu.SMEM)] + [pl.BlockSpec(memory_space=pltpu.VMEM)] * 5
    return pl.pallas_call(
        kernel,
        out_shape=jax.ShapeDtypeStruct((4, 16, 1408), jnp.float32),
        in_specs=specs,
    )(here.reshape(1), order, total, inverses, sums_1, sums_0)


def entered_split(got):
    def kernel(got, pieces, sums_1, sums_0):
        for n in range(4):
            at = slice(256 * n, 256 * n + 256)
            pieces[n] = (got[0, :, at] + got[1, :, at]) + (got[2, :, at] + got[3, :, at])
        for i, out in enumerate((sums_1.at[0], sums_1.at[1], sums_0.at[0])):
            for z in range(4):
                out[:, 128 * z : 128 * z + 128] = got[z, :, 1024 + 128 * i : 1152 + 128 * i]

    return call(kernel, [(4, 16, 256), (2, 16, 512), (1, 16, 512)], got)


def leave_split(target, forward_2, forward_1, forward_0, solution_1, solution_0):
    def kernel(target, forward_2, forward_1, forward_0, solution_1, solution_0, out):
        lane = 0
        for part in (target, forward_2, forward_1, forward_0):
            for n in range(part.shape[0]):
                for z in range(4):
                    out[z, :, lane : lane + 256] = part[n]
                lane += 256
        for part in (solution_0, solution_1):
            for n in range(part.shape[0]):
                for z in range(4):
                    out[z, :, lane : lane + 128] = part[n, :, 128 * z : 128 * z + 128]
                lane += 128

    operands = (target, forward_2, forward_1, forward_0, solution_1, solution_0)
    return call(kernel, [(4, 16, 3200)], *operands)[0]


def left_split(got, inverses):
    def kernel(got, inverses, pieces, forward, solved):
        for n in range(4):
            rounded = got[:, 256 * n : 256 * n + 256].astype(jnp.bfloat16)
            pieces[n] = dot(rounded, inverses[n], 0)
            forward[3 + n] = got[:, 1024 + 256 * n : 1280 + 256 * n]
        for n in range(2):
            forward[1 + n] = got[:, 2048 + 256 * n : 2304 + 256 * n]
        forward[0] = got[:, 2560:2816]
        for n in range(3):
            solved[n] = got[:, 2816 + 128 * n : 2944 + 128 * n]

    shapes = [(4, 64, 128), (7, 64, 256), (3, 64, 128)]
    return call(kernel, shapes, got.reshape(64, 3200), inverses)


def per_device(rhs, factor, inverse, pattern):
    live = pattern.astype(jnp.float32)
    bf16 = jnp.bfloat16
    forward_levels = [None] * LEV
    partial_value = [[] for _ in range(LEV)]

    def push_up(narrow, tree_depth, factors, weights, values):
        count = 2**tree_depth
        for upward in range(1, tree_depth + 1):
            blocks = factors[upward - 1 :: tree_depth]
            terms = product(narrow, blocks, "nrc,nwc->nrw")
            if weights is not None:
                terms = terms * weights[upward - 1 :: tree_depth][:, None, None]
            groups = count >> upward
            terms = terms.reshape((groups, 2**upward) + terms.shape[1:]).sum(axis=1)
            values[tree_depth - upward].append(terms)

    def own_blocks(array, tree_depth):
        start = block_start(tree_depth)
        return array[start : start + 2**tree_depth * tree_depth]

    for tree_depth in range(LEV - 1, TOP - 1, -1):
        residual = nodes_of(rhs, tree_depth)
        if tree_depth < LEV - 1:
            residual = residual - sum_columns(sum(partial_value[tree_depth]))
        pieces = product(residual.astype(bf16), nodes_of(inverse, tree_depth), "nrc,nwc->nrw")
        part = scatter_rows(pieces)
        if tree_depth == LEV - 1:
            whole, part = gather_blocks(inverse[0:3], factor[0:10], part)
        forward = share_rows(part, pieces.shape)
        forward_levels[tree_depth] = forward
        push_up(
            forward.astype(bf16),
            tree_depth,
            own_blocks(factor, tree_depth),
            own_blocks(live, tree_depth),
            partial_value,
        )

    here = (lax.axis_index("pcol") == 0).astype(jnp.float32)
    total = sum_columns(sum(partial_value[2]))
    sent = enter_split(
        rhs[0:7], total, inverse[3:7], sum(partial_value[1]), sum(partial_value[0]), here
    )
    got = lax.all_to_all(sent, "prow", 0, 0, axis_index_groups=ZGROUPS)
    pieces, sums_1, sums_0 = entered_split(got)
    pieces, whole = lax.optimization_barrier((pieces, whole))
    top_inverses = round_inverses(whole, 3)
    top_factors = round_factors(whole, live[0:10], 3)
    top_forward = [None] * TOP
    top_forward[2] = sum_x_ring(pieces)
    top_partial = [[sums_0], [sums_1]]
    inverse_at = [top_inverses[0:1], top_inverses[1:3]]
    factor_at = [None, top_factors[0:2], top_factors[2:10]]
    push_up(top_forward[2].astype(bf16), 2, factor_at[2], None, top_partial)
    for tree_depth in (1, 0):
        residual = -sum_columns(sum(top_partial[tree_depth]))
        pieces = product(residual.astype(bf16), inverse_at[tree_depth], "nrc,nwc->nrw")
        top_forward[tree_depth] = sum_x_ring(pieces)
        if tree_depth:
            push_up(top_forward[1].astype(bf16), 1, factor_at[1], None, top_partial)

    top_solved = []
    for tree_depth in range(TOP):
        target = top_forward[tree_depth]
        if tree_depth:
            terms = 0.0
            for upward in range(tree_depth, 0, -1):
                above = jnp.repeat(
                    top_solved[tree_depth - upward].astype(bf16), 2**upward, axis=0
                )
                blocks = factor_at[tree_depth][upward - 1 :: tree_depth]
                terms = terms + product(above, blocks, "nrw,nwc->nrc")
            target = target - sum_x_ring(terms)
        if tree_depth < TOP - 1:
            pieces = product(target.astype(bf16), inverse_at[tree_depth], "nrw,nwc->nrc")
            top_solved.append(sum_columns(pieces))

    sent = leave_split(target, *top_forward[::-1], top_solved[1], top_solved[0])
    got = lax.all_to_all(sent, "prow", 0, 0, axis_index_groups=ZGROUPS)
    pieces, top_forward, top_solved = left_split(got, inverse[3:7])

    gathered = [[] for _ in range(LEV)]

    def push_down(narrow, tree_depth):
        for lower in range(max(tree_depth + 1, TOP), LEV):
            upward = lower - tree_depth
            above = jnp.repeat(narrow, 2**upward, axis=0)
            terms = product(above, blocks_of(factor, lower, upward), "nrw,nwc->nrc")
            gathered[lower].append(terms * blocks_of(live, lower, upward)[:, None, None])

    for tree_depth in (0, 1):
        push_down(nodes_of(top_solved, tree_depth).astype(bf16), tree_depth)
    solved = [top_solved]
    for tree_depth in range(TOP - 1, LEV):
        if tree_depth >= TOP:
            target = forward_levels[tree_depth] - sum_rows(sum(gathered[tree_depth]))
            pieces = product(target.astype(bf16), nodes_of(inverse, tree_depth), "nrw,nwc->nrc")
        solution = sum_columns(pieces)
        solved.append(solution)
        push_down(solution.astype(bf16), tree_depth)
    forward_levels = [top_forward] + forward_levels[TOP:]
    return (jnp.concatenate(solved, axis=0), jnp.concatenate(forward_levels, axis=0))


def solution(mesh):
    in_specs = (P(None, None, "prow"), P(None, "prow", "pcol"), P(None, "pcol", "prow"), P())
    out_specs = (P(None, None, "prow"), P(None, None, "pcol"))
    return jax.shard_map(
        per_device, mesh=mesh, in_specs=in_specs, out_specs=out_specs, check_vma=False
    )
```

```python
import jax
import jax.numpy as jnp
from jax import lax
from jax.experimental import pallas as pl
from jax.experimental.pallas import tpu as pltpu
from jax.sharding import PartitionSpec as P

LEV = 5
ROWS = 16
TOP = 3
TWIN = [(i, i ^ 1) for i in range(8)]
YRING = [[(i, (i + 2 * k) % 8) for i in range(8)] for k in (2, 1, 3)]
XRING = [[(i, (i + 4 * k) % 16) for i in range(16)] for k in (2, 1, 3)]
ZGROUPS = [[4 * x + z for z in range(4)] for x in range(4)]


def block_start(tree_depth):
    return (tree_depth - 2) * 2**tree_depth + 2


def blocks_of(array, tree_depth, upward):
    start = block_start(tree_depth)
    count = 2**tree_depth
    return array[start + upward - 1 : start + count * tree_depth : tree_depth]


def nodes_of(array, tree_depth):
    return array[2**tree_depth - 1 : 2 ** (tree_depth + 1) - 1]


def product(left, right, form):
    return jnp.einsum(form, left, right, preferred_element_type=jnp.float32)


def sum_children(terms, upward):
    return terms.reshape((-1, 2**upward) + terms.shape[1:]).sum(axis=1)


def top_order(array):
    return jnp.concatenate([array[2:10:2], array[3:10:2], array[0:2]])


def top_inverses(array):
    return jnp.concatenate([array[1:3], array[0:1]])


def sum_ring(values, axis, ring):
    across, right, left = [lax.ppermute(values, axis, step) for step in ring]
    return (values + across) + (right + left)


def sum_columns(values):
    shape = values.shape
    flat = values.reshape(-1, shape[-1])
    if flat.size <= 32768:
        flat = flat + lax.ppermute(flat, "pcol", TWIN)
        return sum_ring(flat, "pcol", YRING).reshape(shape)
    halves = flat.reshape(2, -1, shape[-1])
    core = lax.axis_index("pcol") % 2
    mine = lax.dynamic_index_in_dim(halves, core, 0, keepdims=False)
    other = lax.dynamic_index_in_dim(halves, 1 - core, 0, keepdims=False)
    mine = mine + lax.ppermute(other, "pcol", TWIN)
    mine = sum_ring(mine, "pcol", YRING)
    other = lax.ppermute(mine, "pcol", TWIN)
    both = jnp.where(core == 0, jnp.stack([mine, other]), jnp.stack([other, mine]))
    return both.reshape(shape)


def sum_x_ring(values):
    shape = values.shape
    return sum_ring(values.reshape(-1, shape[-1]), "prow", XRING).reshape(shape)


def scatter_rows(values):
    chunks = values.reshape(ROWS, -1, values.shape[-1])
    return lax.all_to_all(chunks, "prow", 0, 0).sum(axis=0)


def share_rows(part, shape):
    copies = jnp.broadcast_to(part[None], (ROWS,) + part.shape)
    return lax.all_to_all(copies, "prow", 0, 0).reshape(shape)


def sum_rows(values):
    return share_rows(scatter_rows(values), values.shape)


def round_inverses(whole, count, at):
    def kernel(blocks, out):
        for i in range(count):
            for z in range(4):
                out[i, :, 128 * z : 128 * z + 128] = blocks[z, i].astype(jnp.bfloat16)

    return pl.pallas_call(
        kernel,
        out_shape=jax.ShapeDtypeStruct((count, 256, 512), jnp.bfloat16),
        grid=(1,),
        in_specs=[pl.BlockSpec((4, count, 256, 128), lambda i: (0, at, 0, 0))],
        out_specs=pl.BlockSpec((count, 256, 512), lambda i: (0, 0, 0)),
    )(whole)


def round_factors(whole, weights, count, at):
    def kernel(weights, blocks, out):
        for i in range(count):
            for z in range(4):
                for h in range(2):
                    values = blocks[z, i, 128 * h : 128 * h + 128, :] * weights[i]
                    rows = slice(128 * z, 128 * z + 128)
                    out[i, rows, 128 * h : 128 * h + 128] = values.astype(jnp.bfloat16)

    return pl.pallas_call(
        kernel,
        out_shape=jax.ShapeDtypeStruct((count, 512, 256), jnp.bfloat16),
        grid=(1,),
        in_specs=[
            pl.BlockSpec(memory_space=pltpu.SMEM),
            pl.BlockSpec((4, count, 256, 128), lambda i: (0, at, 0, 0)),
        ],
        out_specs=pl.BlockSpec((count, 512, 256), lambda i: (0, 0, 0)),
    )(weights, whole)


def gather_blocks(inverses, factors, after):
    halves = factors.reshape(-1, 128, 2, 128).transpose(0, 2, 1, 3).reshape(-1, 256, 128)
    own = jnp.concatenate([halves, inverses]).astype(jnp.float32)
    own, after = lax.optimization_barrier((own, after))
    whole = lax.all_gather(own, "prow", axis_index_groups=ZGROUPS)
    return whole, after


def call(kernel, shapes, *operands):
    outs = [jax.ShapeDtypeStruct(shape, jnp.float32) for shape in shapes]
    return pl.pallas_call(kernel, out_shape=outs)(*operands)


def dot(left, right, contract):
    dims = (((1,), (contract,)), ((), ()))
    return lax.dot_general(left, right, dims, preferred_element_type=jnp.float32)


def enter_split(order, total, inverses, sums_1, sums_0, here):
    def kernel(here, order, total, inverses, sums_1, sums_0, out):
        for n in range(4):
            rounded = (order[3 + n] - total[n]).astype(jnp.bfloat16)
            piece = dot(rounded, inverses[n], 1)
            for z in range(4):
                out[z, :, 256 * n : 256 * n + 256] = piece[16 * z : 16 * z + 16]
        for i, value in enumerate((sums_1[0], sums_1[1], sums_0[0])):
            value = value - order[(i + 1) % 3] * here[0]
            for z in range(4):
                out[z, :, 1024 + 128 * i : 1152 + 128 * i] = value[16 * z : 16 * z + 16]

    specs = [pl.BlockSpec(memory_space=pltpu.SMEM)] + [pl.BlockSpec(memory_space=pltpu.VMEM)] * 5
    return pl.pallas_call(
        kernel,
        out_shape=jax.ShapeDtypeStruct((4, 16, 1408), jnp.float32),
        in_specs=specs,
    )(here.reshape(1), order, total, inverses, sums_1, sums_0)


def entered_split(got):
    def kernel(got, pieces, sums_1, sums_0):
        for n in range(4):
            at = slice(256 * n, 256 * n + 256)
            pieces[n] = (got[0, :, at] + got[1, :, at]) + (got[2, :, at] + got[3, :, at])
        for i, out in enumerate((sums_1.at[0], sums_1.at[1], sums_0.at[0])):
            for z in range(4):
                out[:, 128 * z : 128 * z + 128] = got[z, :, 1024 + 128 * i : 1152 + 128 * i]

    return call(kernel, [(4, 16, 256), (2, 16, 512), (1, 16, 512)], got)


def leave_split(target, forward_2, forward_1, forward_0, solution_1, solution_0):
    def kernel(target, forward_2, forward_1, forward_0, solution_1, solution_0, out):
        lane = 0
        for part in (target, forward_2, forward_1, forward_0):
            for n in range(part.shape[0]):
                for z in range(4):
                    out[z, :, lane : lane + 256] = part[n]
                lane += 256
        for part in (solution_0, solution_1):
            for n in range(part.shape[0]):
                for z in range(4):
                    out[z, :, lane : lane + 128] = part[n, :, 128 * z : 128 * z + 128]
                lane += 128

    operands = (target, forward_2, forward_1, forward_0, solution_1, solution_0)
    return call(kernel, [(4, 16, 3200)], *operands)[0]


def left_split(got, inverses):
    def kernel(got, inverses, pieces, forward, solved):
        for n in range(4):
            rounded = got[:, 256 * n : 256 * n + 256].astype(jnp.bfloat16)
            pieces[n] = dot(rounded, inverses[n], 0)
            forward[3 + n] = got[:, 1024 + 256 * n : 1280 + 256 * n]
        for n in range(2):
            forward[1 + n] = got[:, 2048 + 256 * n : 2304 + 256 * n]
        forward[0] = got[:, 2560:2816]
        for n in range(3):
            solved[n] = got[:, 2816 + 128 * n : 2944 + 128 * n]

    shapes = [(4, 64, 128), (7, 64, 256), (3, 64, 128)]
    return call(kernel, shapes, got.reshape(64, 3200), inverses)


def per_device(rhs, factor, inverse, pattern):
    live = pattern.astype(jnp.float32)
    bf16 = jnp.bfloat16
    forward_levels = [None] * LEV
    partial_value = [[] for _ in range(LEV)]

    def push_up(narrow, tree_depth):
        for upward in range(1, tree_depth + 1):
            terms = product(narrow, blocks_of(factor, tree_depth, upward), "nrc,nwc->nrw")
            terms = terms * blocks_of(live, tree_depth, upward)[:, None, None]
            partial_value[tree_depth - upward].append(sum_children(terms, upward))

    for tree_depth in range(LEV - 1, TOP - 1, -1):
        residual = nodes_of(rhs, tree_depth)
        if tree_depth < LEV - 1:
            residual = residual - sum_columns(sum(partial_value[tree_depth]))
        pieces = product(residual.astype(bf16), nodes_of(inverse, tree_depth), "nrc,nwc->nrw")
        part = scatter_rows(pieces)
        if tree_depth == LEV - 1:
            whole, part = gather_blocks(top_inverses(inverse), top_order(factor), part)
        forward = share_rows(part, pieces.shape)
        forward_levels[tree_depth] = forward
        push_up(forward.astype(bf16), tree_depth)

    here = (lax.axis_index("pcol") == 0).astype(jnp.float32)
    total = sum_columns(sum(partial_value[2]))
    sent = enter_split(
        rhs[0:7], total, inverse[3:7], sum(partial_value[1]), sum(partial_value[0]), here
    )
    got = lax.all_to_all(sent, "prow", 0, 0, axis_index_groups=ZGROUPS)
    pieces, sums_1, sums_0 = entered_split(got)
    pieces, whole = lax.optimization_barrier((pieces, whole))
    weights = top_order(live)
    parents = round_factors(whole, weights[0:4], 4, 0)
    roots = round_factors(whole, weights[4:8], 4, 1)
    children = round_factors(whole, weights[8:10], 2, 4)
    inverse_at = [round_inverses(whole, 1, 12), round_inverses(whole, 2, 5)]
    top_forward = [None] * TOP
    top_forward[2] = sum_x_ring(pieces)
    top_partial = [[sums_0], [sums_1]]

    def split_up(narrow, tree_depth):
        for upward in range(1, tree_depth + 1):
            terms = product(narrow, factor_at[tree_depth][upward - 1], "nrc,nwc->nrw")
            top_partial[tree_depth - upward].append(sum_children(terms, upward))

    factor_at = [None, [children], [parents, roots]]
    split_up(top_forward[2].astype(bf16), 2)
    for tree_depth in (1, 0):
        residual = -sum_columns(sum(top_partial[tree_depth]))
        pieces = product(residual.astype(bf16), inverse_at[tree_depth], "nrc,nwc->nrw")
        top_forward[tree_depth] = sum_x_ring(pieces)
        if tree_depth:
            split_up(top_forward[1].astype(bf16), 1)

    top_solved = []
    for tree_depth in range(TOP):
        target = top_forward[tree_depth]
        if tree_depth:
            terms = 0.0
            for upward in range(tree_depth, 0, -1):
                above = jnp.repeat(
                    top_solved[tree_depth - upward].astype(bf16), 2**upward, axis=0
                )
                blocks = factor_at[tree_depth][upward - 1]
                terms = terms + product(above, blocks, "nrw,nwc->nrc")
            target = target - sum_x_ring(terms)
        if tree_depth < TOP - 1:
            pieces = product(target.astype(bf16), inverse_at[tree_depth], "nrw,nwc->nrc")
            top_solved.append(sum_columns(pieces))

    sent = leave_split(target, *top_forward[::-1], top_solved[1], top_solved[0])
    got = lax.all_to_all(sent, "prow", 0, 0, axis_index_groups=ZGROUPS)
    pieces, top_forward, top_solved = left_split(got, inverse[3:7])

    gathered = [[] for _ in range(LEV)]

    def push_down(narrow, tree_depth):
        for lower in range(max(tree_depth + 1, TOP), LEV):
            upward = lower - tree_depth
            above = jnp.repeat(narrow, 2**upward, axis=0)
            terms = product(above, blocks_of(factor, lower, upward), "nrw,nwc->nrc")
            gathered[lower].append(terms * blocks_of(live, lower, upward)[:, None, None])

    for tree_depth in (0, 1):
        push_down(nodes_of(top_solved, tree_depth).astype(bf16), tree_depth)
    solved = [top_solved]
    for tree_depth in range(TOP - 1, LEV):
        if tree_depth >= TOP:
            target = forward_levels[tree_depth] - sum_rows(sum(gathered[tree_depth]))
            if tree_depth == LEV - 1:
                forward_whole = jnp.concatenate([top_forward] + forward_levels[TOP:])
                target, forward_whole = lax.optimization_barrier((target, forward_whole))
            pieces = product(target.astype(bf16), nodes_of(inverse, tree_depth), "nrw,nwc->nrc")
        solution = sum_columns(pieces)
        solved.append(solution)
        push_down(solution.astype(bf16), tree_depth)
    return jnp.concatenate(solved), forward_whole


def solution(mesh):
    in_specs = (P(None, None, "prow"), P(None, "prow", "pcol"), P(None, "pcol", "prow"), P())
    out_specs = (P(None, None, "prow"), P(None, None, "pcol"))
    return jax.shard_map(
        per_device, mesh=mesh, in_specs=in_specs, out_specs=out_specs, check_vma=False
    )
```

```python
import jax
import jax.numpy as jnp
from jax import lax
from jax.experimental import pallas as pl
from jax.experimental.pallas import tpu as pltpu
from jax.sharding import PartitionSpec as P

LEV = 5
ROWS = 16
TOP = 3
TWIN = [(i, i ^ 1) for i in range(8)]
YRING = [[(i, (i + 2 * k) % 8) for i in range(8)] for k in (2, 1, 3)]
XRING = [[(i, (i + 4 * k) % 16) for i in range(16)] for k in (2, 1, 3)]
ZGROUPS = [[4 * x + z for z in range(4)] for x in range(4)]


def block_start(tree_depth):
    return (tree_depth - 2) * 2**tree_depth + 2


def blocks_of(array, tree_depth, upward):
    start = block_start(tree_depth)
    count = 2**tree_depth
    return array[start + upward - 1 : start + count * tree_depth : tree_depth]


def nodes_of(array, tree_depth):
    return array[2**tree_depth - 1 : 2 ** (tree_depth + 1) - 1]


def product(left, right, form):
    return jnp.einsum(form, left, right, preferred_element_type=jnp.float32)


def sum_children(terms, upward):
    return terms.reshape((-1, 2**upward) + terms.shape[1:]).sum(axis=1)


def top_order(array):
    return jnp.concatenate([array[2:10:2], array[3:10:2], array[0:2]])


def top_inverses(array):
    return jnp.concatenate([array[1:3], array[0:1]])


def sum_ring(values, axis, ring):
    across, right, left = [lax.ppermute(values, axis, step) for step in ring]
    return (values + across) + (right + left)


def sum_columns(values):
    shape = values.shape
    flat = values.reshape(-1, shape[-1])
    if flat.size <= 32768:
        flat = flat + lax.ppermute(flat, "pcol", TWIN)
        return sum_ring(flat, "pcol", YRING).reshape(shape)
    halves = flat.reshape(2, -1, shape[-1])
    core = lax.axis_index("pcol") % 2
    mine = lax.dynamic_index_in_dim(halves, core, 0, keepdims=False)
    other = lax.dynamic_index_in_dim(halves, 1 - core, 0, keepdims=False)
    mine = mine + lax.ppermute(other, "pcol", TWIN)
    mine = sum_ring(mine, "pcol", YRING)
    other = lax.ppermute(mine, "pcol", TWIN)
    both = jnp.where(core == 0, jnp.stack([mine, other]), jnp.stack([other, mine]))
    return both.reshape(shape)


def sum_x_ring(values):
    shape = values.shape
    return sum_ring(values.reshape(-1, shape[-1]), "prow", XRING).reshape(shape)


def scatter_rows(values):
    chunks = values.reshape(ROWS, -1, values.shape[-1])
    return lax.all_to_all(chunks, "prow", 0, 0).sum(axis=0)


def share_rows(part, shape):
    copies = jnp.broadcast_to(part[None], (ROWS,) + part.shape)
    return lax.all_to_all(copies, "prow", 0, 0).reshape(shape)


def sum_rows(values):
    return share_rows(scatter_rows(values), values.shape)


def resident(array, first, last, step):
    blocks = range(first, last, step)

    def kernel(source, target, arrived):
        copies = [
            pltpu.make_async_copy(source.at[block], target.at[i], arrived.at[i])
            for i, block in enumerate(blocks)
        ]
        for copy in copies:
            copy.start()
        for copy in copies:
            copy.wait()

    return pl.pallas_call(
        kernel,
        out_shape=pltpu.VMEM((len(blocks),) + array.shape[1:], array.dtype),
        in_specs=[pl.BlockSpec(memory_space=pltpu.HBM)],
        out_specs=pl.BlockSpec(memory_space=pltpu.VMEM),
        scratch_shapes=[pltpu.SemaphoreType.DMA((len(blocks),))],
        compiler_params=pltpu.CompilerParams(vmem_limit_bytes=4 << 20),
    )(array)


def round_inverses(whole, count, at):
    def kernel(blocks, out):
        for i in range(count):
            for z in range(4):
                out[i, :, 128 * z : 128 * z + 128] = blocks[z, i].astype(jnp.bfloat16)

    return pl.pallas_call(
        kernel,
        out_shape=pltpu.VMEM((count, 256, 512), jnp.bfloat16),
        grid=(1,),
        in_specs=[pl.BlockSpec((4, count, 256, 128), lambda i: (0, at, 0, 0))],
        out_specs=pl.BlockSpec((count, 256, 512), lambda i: (0, 0, 0)),
    )(whole)


def round_factors(whole, weights, count, at):
    def kernel(weights, blocks, out):
        for i in range(count):
            for z in range(4):
                for h in range(2):
                    values = blocks[z, i, 128 * h : 128 * h + 128, :] * weights[i]
                    rows = slice(128 * z, 128 * z + 128)
                    out[i, rows, 128 * h : 128 * h + 128] = values.astype(jnp.bfloat16)

    return pl.pallas_call(
        kernel,
        out_shape=pltpu.VMEM((count, 512, 256), jnp.bfloat16),
        grid=(1,),
        in_specs=[
            pl.BlockSpec(memory_space=pltpu.SMEM),
            pl.BlockSpec((4, count, 256, 128), lambda i: (0, at, 0, 0)),
        ],
        out_specs=pl.BlockSpec((count, 512, 256), lambda i: (0, 0, 0)),
    )(weights, whole)


def gather_blocks(inverses, factors, after):
    halves = factors.reshape(-1, 128, 2, 128).transpose(0, 2, 1, 3).reshape(-1, 256, 128)
    own = jnp.concatenate([halves, inverses]).astype(jnp.float32)
    own, after = lax.optimization_barrier((own, after))
    whole = lax.all_gather(own, "prow", axis_index_groups=ZGROUPS)
    return whole, after


def call(kernel, shapes, *operands):
    outs = [pltpu.VMEM(shape, jnp.float32) for shape in shapes]
    return pl.pallas_call(kernel, out_shape=outs)(*operands)


def dot(left, right, contract):
    dims = (((1,), (contract,)), ((), ()))
    return lax.dot_general(left, right, dims, preferred_element_type=jnp.float32)


def enter_split(order, total, inverses, sums_1, sums_0, here):
    def kernel(here, order, total, inverses, sums_1, sums_0, out):
        for n in range(4):
            rounded = (order[3 + n] - total[n]).astype(jnp.bfloat16)
            piece = dot(rounded, inverses[n], 1)
            for z in range(4):
                out[z, :, 256 * n : 256 * n + 256] = piece[16 * z : 16 * z + 16]
        for i, value in enumerate((sums_1[0], sums_1[1], sums_0[0])):
            value = value - order[(i + 1) % 3] * here[0]
            for z in range(4):
                out[z, :, 1024 + 128 * i : 1152 + 128 * i] = value[16 * z : 16 * z + 16]

    specs = [pl.BlockSpec(memory_space=pltpu.SMEM)] + [pl.BlockSpec(memory_space=pltpu.VMEM)] * 5
    return pl.pallas_call(
        kernel,
        out_shape=pltpu.VMEM((4, 16, 1408), jnp.float32),
        in_specs=specs,
    )(here.reshape(1), order, total, inverses, sums_1, sums_0)


def entered_split(got):
    def kernel(got, pieces, sums_1, sums_0):
        for n in range(4):
            at = slice(256 * n, 256 * n + 256)
            pieces[n] = (got[0, :, at] + got[1, :, at]) + (got[2, :, at] + got[3, :, at])
        for i, out in enumerate((sums_1.at[0], sums_1.at[1], sums_0.at[0])):
            for z in range(4):
                out[:, 128 * z : 128 * z + 128] = got[z, :, 1024 + 128 * i : 1152 + 128 * i]

    return call(kernel, [(4, 16, 256), (2, 16, 512), (1, 16, 512)], got)


def leave_split(target, forward_2, forward_1, forward_0, solution_1, solution_0):
    def kernel(target, forward_2, forward_1, forward_0, solution_1, solution_0, out):
        lane = 0
        for part in (target, forward_2, forward_1, forward_0):
            for n in range(part.shape[0]):
                for z in range(4):
                    out[z, :, lane : lane + 256] = part[n]
                lane += 256
        for part in (solution_0, solution_1):
            for n in range(part.shape[0]):
                for z in range(4):
                    out[z, :, lane : lane + 128] = part[n, :, 128 * z : 128 * z + 128]
                lane += 128

    operands = (target, forward_2, forward_1, forward_0, solution_1, solution_0)
    return call(kernel, [(4, 16, 3200)], *operands)[0]


def left_split(got, inverses):
    def kernel(got, inverses, pieces, forward, solved):
        for n in range(4):
            rounded = got[:, 256 * n : 256 * n + 256].astype(jnp.bfloat16)
            pieces[n] = dot(rounded, inverses[n], 0)
            forward[3 + n] = got[:, 1024 + 256 * n : 1280 + 256 * n]
        for n in range(2):
            forward[1 + n] = got[:, 2048 + 256 * n : 2304 + 256 * n]
        forward[0] = got[:, 2560:2816]
        for n in range(3):
            solved[n] = got[:, 2816 + 128 * n : 2944 + 128 * n]

    shapes = [(4, 64, 128), (7, 64, 256), (3, 64, 128)]
    return call(kernel, shapes, got.reshape(64, 3200), inverses)


def per_device(rhs, factor, inverse, pattern):
    live = pattern.astype(jnp.float32)
    bf16 = jnp.bfloat16
    forward_levels = [None] * LEV
    far = (inverse, factor)
    partial_value = [[] for _ in range(LEV)]

    def push_up(narrow, tree_depth):
        for upward in range(1, tree_depth + 1):
            blocks = parent_at[tree_depth] if upward == 1 else blocks_of(factor, tree_depth, upward)
            terms = product(narrow, blocks, "nrc,nwc->nrw")
            terms = terms * blocks_of(live, tree_depth, upward)[:, None, None]
            partial_value[tree_depth - upward].append(sum_children(terms, upward))

    for tree_depth in range(LEV - 1, TOP - 1, -1):
        residual = nodes_of(rhs, tree_depth)
        if tree_depth < LEV - 1:
            residual = residual - sum_columns(sum(partial_value[tree_depth]))
        pieces = product(residual.astype(bf16), nodes_of(inverse, tree_depth), "nrc,nwc->nrw")
        if tree_depth == LEV - 1:
            pieces, near, inverse = lax.optimization_barrier((pieces, factor, inverse))
            inverse = resident(inverse, 0, 31, 1)
            parent_at = {4: resident(near, 34, 98, 4), 3: resident(near, 10, 34, 3)}
        part = scatter_rows(pieces)
        if tree_depth == LEV - 1:
            whole, part = gather_blocks(top_inverses(far[0]), top_order(far[1]), part)
        forward = share_rows(part, pieces.shape)
        forward_levels[tree_depth] = forward
        push_up(forward.astype(bf16), tree_depth)

    here = (lax.axis_index("pcol") == 0).astype(jnp.float32)
    total = sum_columns(sum(partial_value[2]))
    sent = enter_split(
        rhs[0:7], total, inverse[3:7], sum(partial_value[1]), sum(partial_value[0]), here
    )
    got = lax.all_to_all(sent, "prow", 0, 0, axis_index_groups=ZGROUPS)
    pieces, sums_1, sums_0 = entered_split(got)
    pieces, whole = lax.optimization_barrier((pieces, whole))
    weights = top_order(live)
    parents = round_factors(whole, weights[0:4], 4, 0)
    roots = round_factors(whole, weights[4:8], 4, 1)
    children = round_factors(whole, weights[8:10], 2, 4)
    inverse_at = [round_inverses(whole, 1, 12), round_inverses(whole, 2, 5)]
    top_forward = [None] * TOP
    top_forward[2] = sum_x_ring(pieces)
    top_partial = [[sums_0], [sums_1]]

    def split_up(narrow, tree_depth):
        for upward in range(1, tree_depth + 1):
            terms = product(narrow, factor_at[tree_depth][upward - 1], "nrc,nwc->nrw")
            top_partial[tree_depth - upward].append(sum_children(terms, upward))

    factor_at = [None, [children], [parents, roots]]
    split_up(top_forward[2].astype(bf16), 2)
    for tree_depth in (1, 0):
        residual = -sum_columns(sum(top_partial[tree_depth]))
        pieces = product(residual.astype(bf16), inverse_at[tree_depth], "nrc,nwc->nrw")
        top_forward[tree_depth] = sum_x_ring(pieces)
        if tree_depth:
            split_up(top_forward[1].astype(bf16), 1)

    top_solved = []
    for tree_depth in range(TOP):
        target = top_forward[tree_depth]
        if tree_depth:
            terms = 0.0
            for upward in range(tree_depth, 0, -1):
                above = jnp.repeat(
                    top_solved[tree_depth - upward].astype(bf16), 2**upward, axis=0
                )
                blocks = factor_at[tree_depth][upward - 1]
                terms = terms + product(above, blocks, "nrw,nwc->nrc")
            target = target - sum_x_ring(terms)
        if tree_depth < TOP - 1:
            pieces = product(target.astype(bf16), inverse_at[tree_depth], "nrw,nwc->nrc")
            top_solved.append(sum_columns(pieces))

    sent = leave_split(target, *top_forward[::-1], top_solved[1], top_solved[0])
    got = lax.all_to_all(sent, "prow", 0, 0, axis_index_groups=ZGROUPS)
    pieces, top_forward, top_solved = left_split(got, inverse[3:7])

    gathered = [[] for _ in range(LEV)]

    def push_down(narrow, tree_depth):
        for lower in range(max(tree_depth + 1, TOP), LEV):
            upward = lower - tree_depth
            above = jnp.repeat(narrow, 2**upward, axis=0)
            blocks = parent_at[lower] if upward == 1 else blocks_of(factor, lower, upward)
            terms = product(above, blocks, "nrw,nwc->nrc")
            gathered[lower].append(terms * blocks_of(live, lower, upward)[:, None, None])

    for tree_depth in (0, 1):
        push_down(nodes_of(top_solved, tree_depth).astype(bf16), tree_depth)
    solved = [top_solved]
    for tree_depth in range(TOP - 1, LEV):
        if tree_depth >= TOP:
            target = forward_levels[tree_depth] - sum_rows(sum(gathered[tree_depth]))
            if tree_depth == LEV - 1:
                forward_whole = jnp.concatenate([top_forward] + forward_levels[TOP:])
                target, forward_whole = lax.optimization_barrier((target, forward_whole))
            pieces = product(target.astype(bf16), nodes_of(inverse, tree_depth), "nrw,nwc->nrc")
        solution = sum_columns(pieces)
        solved.append(solution)
        push_down(solution.astype(bf16), tree_depth)
    return jnp.concatenate(solved), forward_whole


def solution(mesh):
    in_specs = (P(None, None, "prow"), P(None, "prow", "pcol"), P(None, "pcol", "prow"), P())
    out_specs = (P(None, None, "prow"), P(None, None, "pcol"))
    return jax.shard_map(
        per_device, mesh=mesh, in_specs=in_specs, out_specs=out_specs, check_vma=False
    )
```

```python
import jax
import jax.numpy as jnp
from jax import lax
from jax.experimental import pallas as pl
from jax.experimental.pallas import tpu as pltpu
from jax.sharding import PartitionSpec as P

LEV = 5
ROWS = 16
TOP = 3
TWIN = [(i, i ^ 1) for i in range(8)]
YRING = [[(i, (i + 2 * k) % 8) for i in range(8)] for k in (2, 1, 3)]
XRING = [[(i, (i + 4 * k) % 16) for i in range(16)] for k in (2, 1, 3)]
ZGROUPS = [[4 * x + z for z in range(4)] for x in range(4)]


def block_start(tree_depth):
    return (tree_depth - 2) * 2**tree_depth + 2


def blocks_of(array, tree_depth, upward):
    start = block_start(tree_depth)
    count = 2**tree_depth
    return array[start + upward - 1 : start + count * tree_depth : tree_depth]


def nodes_of(array, tree_depth):
    return array[2**tree_depth - 1 : 2 ** (tree_depth + 1) - 1]


def product(left, right, form):
    return jnp.einsum(form, left, right, preferred_element_type=jnp.float32)


def sum_children(terms, upward):
    return terms.reshape((-1, 2**upward) + terms.shape[1:]).sum(axis=1)


def top_order(array):
    return jnp.concatenate([array[2:10:2], array[3:10:2], array[0:2]])


def top_inverses(array):
    return jnp.concatenate([array[1:3], array[0:1]])


def sum_ring(values, axis, ring):
    across, right, left = [lax.ppermute(values, axis, step) for step in ring]
    return (values + across) + (right + left)


def sum_columns(values):
    shape = values.shape
    flat = values.reshape(-1, shape[-1])
    if flat.size <= 32768:
        flat = flat + lax.ppermute(flat, "pcol", TWIN)
        return sum_ring(flat, "pcol", YRING).reshape(shape)
    halves = flat.reshape(2, -1, shape[-1])
    core = lax.axis_index("pcol") % 2
    mine = lax.dynamic_index_in_dim(halves, core, 0, keepdims=False)
    other = lax.dynamic_index_in_dim(halves, 1 - core, 0, keepdims=False)
    mine = mine + lax.ppermute(other, "pcol", TWIN)
    mine = sum_ring(mine, "pcol", YRING)
    other = lax.ppermute(mine, "pcol", TWIN)
    both = jnp.where(core == 0, jnp.stack([mine, other]), jnp.stack([other, mine]))
    return both.reshape(shape)


def sum_x_ring(values):
    shape = values.shape
    return sum_ring(values.reshape(-1, shape[-1]), "prow", XRING).reshape(shape)


def scatter_rows(values):
    chunks = values.reshape(ROWS, -1, values.shape[-1])
    return lax.all_to_all(chunks, "prow", 0, 0)


def share_rows(parts, shape):
    def kernel(parts, out):
        total = parts[0]
        for i in range(1, ROWS):
            total = total + parts[i]
        for i in range(ROWS):
            out[i] = total

    copies = call(kernel, [parts.shape], parts)[0]
    return lax.all_to_all(copies, "prow", 0, 0).reshape(shape)


def sum_rows(values):
    return share_rows(scatter_rows(values), values.shape)


def resident(array, *ranges):
    total = sum(len(blocks) for blocks in ranges)

    def kernel(source, *refs):
        arrived = refs[-1]
        copies = []
        for target, blocks in zip(refs, ranges):
            for i, block in enumerate(blocks):
                at = arrived.at[len(copies)]
                copies.append(pltpu.make_async_copy(source.at[block], target.at[i], at))
        for copy in copies:
            copy.start()
        for copy in copies:
            copy.wait()

    return pl.pallas_call(
        kernel,
        out_shape=[pltpu.VMEM((len(blocks),) + array.shape[1:], array.dtype) for blocks in ranges],
        in_specs=[pl.BlockSpec(memory_space=pltpu.HBM)],
        out_specs=[pl.BlockSpec(memory_space=pltpu.VMEM)] * len(ranges),
        scratch_shapes=[pltpu.SemaphoreType.DMA((total,))],
        compiler_params=pltpu.CompilerParams(vmem_limit_bytes=4 << 20),
    )(array)


def round_inverses(whole, count, at):
    def kernel(blocks, out):
        for i in range(count):
            for z in range(4):
                out[i, :, 128 * z : 128 * z + 128] = blocks[z, i].astype(jnp.bfloat16)

    return pl.pallas_call(
        kernel,
        out_shape=pltpu.VMEM((count, 256, 512), jnp.bfloat16),
        grid=(1,),
        in_specs=[pl.BlockSpec((4, count, 256, 128), lambda i: (0, at, 0, 0))],
        out_specs=pl.BlockSpec((count, 256, 512), lambda i: (0, 0, 0)),
    )(whole)


def round_factors(whole, weights, count, at):
    def kernel(weights, blocks, out):
        for i in range(count):
            for z in range(4):
                for h in range(2):
                    values = blocks[z, i, 128 * h : 128 * h + 128, :] * weights[i]
                    rows = slice(128 * z, 128 * z + 128)
                    out[i, rows, 128 * h : 128 * h + 128] = values.astype(jnp.bfloat16)

    return pl.pallas_call(
        kernel,
        out_shape=pltpu.VMEM((count, 512, 256), jnp.bfloat16),
        grid=(1,),
        in_specs=[
            pl.BlockSpec(memory_space=pltpu.SMEM),
            pl.BlockSpec((4, count, 256, 128), lambda i: (0, at, 0, 0)),
        ],
        out_specs=pl.BlockSpec((count, 512, 256), lambda i: (0, 0, 0)),
    )(weights, whole)


def gather_blocks(inverses, factors, after):
    halves = factors.reshape(-1, 128, 2, 128).transpose(0, 2, 1, 3).reshape(-1, 256, 128)
    own = jnp.concatenate([halves, inverses]).astype(jnp.float32)
    own, after = lax.optimization_barrier((own, after))
    whole = lax.all_gather(own, "prow", axis_index_groups=ZGROUPS)
    return whole, after


def call(kernel, shapes, *operands):
    outs = [pltpu.VMEM(shape, jnp.float32) for shape in shapes]
    return pl.pallas_call(kernel, out_shape=outs)(*operands)


def dot(left, right, contract):
    dims = (((1,), (contract,)), ((), ()))
    return lax.dot_general(left, right, dims, preferred_element_type=jnp.float32)


def enter_split(order, total, inverses, sums_1, sums_0, here):
    def kernel(here, order, total, inverses, sums_1, sums_0, out):
        for n in range(4):
            rounded = (order[3 + n] - total[n]).astype(jnp.bfloat16)
            piece = dot(rounded, inverses[n], 1)
            for z in range(4):
                out[z, :, 256 * n : 256 * n + 256] = piece[16 * z : 16 * z + 16]
        for i, value in enumerate((sums_1[0], sums_1[1], sums_0[0])):
            value = value - order[(i + 1) % 3] * here[0]
            for z in range(4):
                out[z, :, 1024 + 128 * i : 1152 + 128 * i] = value[16 * z : 16 * z + 16]

    specs = [pl.BlockSpec(memory_space=pltpu.SMEM)] + [pl.BlockSpec(memory_space=pltpu.VMEM)] * 5
    return pl.pallas_call(
        kernel,
        out_shape=pltpu.VMEM((4, 16, 1408), jnp.float32),
        in_specs=specs,
    )(here.reshape(1), order, total, inverses, sums_1, sums_0)


def entered_split(got):
    def kernel(got, pieces, sums_1, sums_0):
        for n in range(4):
            at = slice(256 * n, 256 * n + 256)
            pieces[n] = (got[0, :, at] + got[1, :, at]) + (got[2, :, at] + got[3, :, at])
        for i, out in enumerate((sums_1.at[0], sums_1.at[1], sums_0.at[0])):
            for z in range(4):
                out[:, 128 * z : 128 * z + 128] = got[z, :, 1024 + 128 * i : 1152 + 128 * i]

    return call(kernel, [(4, 16, 256), (2, 16, 512), (1, 16, 512)], got)


def leave_split(target, forward_2, forward_1, forward_0, solution_1, solution_0):
    def kernel(target, forward_2, forward_1, forward_0, solution_1, solution_0, out):
        lane = 0
        for part in (target, forward_2, forward_1, forward_0):
            for n in range(part.shape[0]):
                for z in range(4):
                    out[z, :, lane : lane + 256] = part[n]
                lane += 256
        for part in (solution_0, solution_1):
            for n in range(part.shape[0]):
                for z in range(4):
                    out[z, :, lane : lane + 128] = part[n, :, 128 * z : 128 * z + 128]
                lane += 128

    operands = (target, forward_2, forward_1, forward_0, solution_1, solution_0)
    return call(kernel, [(4, 16, 3200)], *operands)[0]


def left_split(got, inverses):
    def kernel(got, inverses, pieces, forward, solved):
        for n in range(4):
            rounded = got[:, 256 * n : 256 * n + 256].astype(jnp.bfloat16)
            pieces[n] = dot(rounded, inverses[n], 0)
            forward[3 + n] = got[:, 1024 + 256 * n : 1280 + 256 * n]
        for n in range(2):
            forward[1 + n] = got[:, 2048 + 256 * n : 2304 + 256 * n]
        forward[0] = got[:, 2560:2816]
        for n in range(3):
            solved[n] = got[:, 2816 + 128 * n : 2944 + 128 * n]

    shapes = [(4, 64, 128), (7, 64, 256), (3, 64, 128)]
    return call(kernel, shapes, got.reshape(64, 3200), inverses)


def per_device(rhs, factor, inverse, pattern):
    live = pattern.astype(jnp.float32)
    bf16 = jnp.bfloat16
    forward_levels = [None] * LEV
    far = (inverse, factor)
    partial_value = [[] for _ in range(LEV)]

    def push_up(narrow, tree_depth, first, last):
        for upward in range(first, last + 1):
            blocks = parent_at[tree_depth] if upward == 1 else blocks_of(factor, tree_depth, upward)
            terms = product(narrow, blocks, "nrc,nwc->nrw")
            terms = terms * blocks_of(live, tree_depth, upward)[:, None, None]
            partial_value[tree_depth - upward].append(sum_children(terms, upward))

    for tree_depth in range(LEV - 1, TOP - 1, -1):
        if tree_depth == LEV - 1:
            residual = nodes_of(rhs, tree_depth)
            blocks = nodes_of(inverse, tree_depth)
        else:
            residual = order[0] - sum_columns(sum(partial_value[tree_depth]))
            blocks = inverses[0]
        pieces = product(residual.astype(bf16), blocks, "nrc,nwc->nrw")
        if tree_depth == LEV - 1:
            near = lax.optimization_barrier((pieces, factor, inverse, rhs))
            pieces = near[0]
            parents = resident(near[1], range(34, 98, 4), range(10, 34, 3))
            inverses = resident(near[2], range(7, 15), range(3, 7))
            order = resident(near[3], range(7, 15))
        part = scatter_rows(pieces)
        if tree_depth == LEV - 1:
            part, parents, inverses, order = lax.optimization_barrier(
                (part, parents, inverses, order)
            )
            parent_at = {4: parents[0], 3: parents[1]}
            whole, part = gather_blocks(top_inverses(far[0]), top_order(far[1]), part)
        forward = share_rows(part, pieces.shape)
        forward_levels[tree_depth] = forward
        narrow = forward.astype(bf16)
        push_up(narrow, tree_depth, 1, tree_depth if tree_depth > TOP else 1)

    here = (lax.axis_index("pcol") == 0).astype(jnp.float32)
    total = sum(partial_value[2]).reshape(-1, 128)
    total = total + lax.ppermute(total, "pcol", TWIN)
    total, narrow = lax.optimization_barrier((total, narrow))
    total = sum_ring(total, "pcol", YRING).reshape(4, 64, 128)
    push_up(narrow, TOP, 2, TOP)
    sent = enter_split(
        rhs[0:7], total, inverses[1], sum(partial_value[1]), sum(partial_value[0]), here
    )
    got = lax.all_to_all(sent, "prow", 0, 0, axis_index_groups=ZGROUPS)
    pieces, sums_1, sums_0 = entered_split(got)
    pieces, whole = lax.optimization_barrier((pieces, whole))
    weights = top_order(live)
    parents = round_factors(whole, weights[0:4], 4, 0)
    roots = round_factors(whole, weights[4:8], 4, 1)
    children = round_factors(whole, weights[8:10], 2, 4)
    inverse_at = [round_inverses(whole, 1, 12), round_inverses(whole, 2, 5)]
    top_forward = [None] * TOP
    top_forward[2] = sum_x_ring(pieces)
    top_partial = [[sums_0], [sums_1]]

    def split_up(narrow, tree_depth):
        for upward in range(1, tree_depth + 1):
            terms = product(narrow, factor_at[tree_depth][upward - 1], "nrc,nwc->nrw")
            top_partial[tree_depth - upward].append(sum_children(terms, upward))

    factor_at = [None, [children], [parents, roots]]
    split_up(top_forward[2].astype(bf16), 2)
    for tree_depth in (1, 0):
        residual = -sum_columns(sum(top_partial[tree_depth]))
        pieces = product(residual.astype(bf16), inverse_at[tree_depth], "nrc,nwc->nrw")
        top_forward[tree_depth] = sum_x_ring(pieces)
        if tree_depth:
            split_up(top_forward[1].astype(bf16), 1)

    top_solved = []
    for tree_depth in range(TOP):
        target = top_forward[tree_depth]
        if tree_depth:
            terms = 0.0
            for upward in range(tree_depth, 0, -1):
                above = jnp.repeat(
                    top_solved[tree_depth - upward].astype(bf16), 2**upward, axis=0
                )
                blocks = factor_at[tree_depth][upward - 1]
                terms = terms + product(above, blocks, "nrw,nwc->nrc")
            target = target - sum_x_ring(terms)
        if tree_depth < TOP - 1:
            pieces = product(target.astype(bf16), inverse_at[tree_depth], "nrw,nwc->nrc")
            top_solved.append(sum_columns(pieces))

    sent = leave_split(target, *top_forward[::-1], top_solved[1], top_solved[0])
    got = lax.all_to_all(sent, "prow", 0, 0, axis_index_groups=ZGROUPS)
    pieces, top_forward, top_solved = left_split(got, inverses[1])

    gathered = [[] for _ in range(LEV)]

    def push_down(narrow, tree_depth):
        for lower in range(max(tree_depth + 1, TOP), LEV):
            upward = lower - tree_depth
            above = jnp.repeat(narrow, 2**upward, axis=0)
            blocks = parent_at[lower] if upward == 1 else blocks_of(factor, lower, upward)
            terms = product(above, blocks, "nrw,nwc->nrc")
            gathered[lower].append(terms * blocks_of(live, lower, upward)[:, None, None])

    for tree_depth in (0, 1):
        push_down(nodes_of(top_solved, tree_depth).astype(bf16), tree_depth)
    solved = [top_solved]
    for tree_depth in range(TOP - 1, LEV):
        if tree_depth >= TOP:
            target = forward_levels[tree_depth] - sum_rows(sum(gathered[tree_depth]))
            if tree_depth == LEV - 1:
                forward_whole = jnp.concatenate([top_forward] + forward_levels[TOP:])
                upper = jnp.zeros(rhs.shape, jnp.float32).at[:15].set(jnp.concatenate(solved))
                target, forward_whole, upper = lax.optimization_barrier(
                    (target, forward_whole, upper)
                )
            blocks = inverses[0] if tree_depth == TOP else nodes_of(inverse, tree_depth)
            pieces = product(target.astype(bf16), blocks, "nrw,nwc->nrc")
        solution = sum_columns(pieces)
        solved.append(solution)
        push_down(solution.astype(bf16), tree_depth)
    return upper.at[15:].set(solved[-1]), forward_whole


def solution(mesh):
    in_specs = (P(None, None, "prow"), P(None, "prow", "pcol"), P(None, "pcol", "prow"), P())
    out_specs = (P(None, None, "prow"), P(None, None, "pcol"))
    return jax.shard_map(
        per_device, mesh=mesh, in_specs=in_specs, out_specs=out_specs, check_vma=False
    )
```

```python
import jax
import jax.numpy as jnp
from jax import lax
from jax.experimental import pallas as pl
from jax.experimental.pallas import tpu as pltpu
from jax.sharding import PartitionSpec as P

LEV = 5
ROWS = 16
TOP = 3
TWIN = [(i, i ^ 1) for i in range(8)]
YRING = [[(i, (i + 2 * k) % 8) for i in range(8)] for k in (2, 1, 3)]
XRING = [[(i, (i + 4 * k) % 16) for i in range(16)] for k in (2, 1, 3)]
ZGROUPS = [[4 * x + z for z in range(4)] for x in range(4)]


def block_start(tree_depth):
    return (tree_depth - 2) * 2**tree_depth + 2


def blocks_of(array, tree_depth, upward):
    start = block_start(tree_depth)
    count = 2**tree_depth
    return array[start + upward - 1 : start + count * tree_depth : tree_depth]


def nodes_of(array, tree_depth):
    return array[2**tree_depth - 1 : 2 ** (tree_depth + 1) - 1]


def product(left, right, form):
    return jnp.einsum(form, left, right, preferred_element_type=jnp.float32)


def grant(megabytes):
    return pltpu.CompilerParams(vmem_limit_bytes=megabytes << 20)


def sum_children(terms, upward):
    return terms.reshape((-1, 2**upward) + terms.shape[1:]).sum(axis=1)


def top_order(array):
    return jnp.concatenate([array[2:10:2], array[3:10:2], array[0:2]])


def top_inverses(array):
    return jnp.concatenate([array[1:3], array[0:1]])


def sum_ring(values, axis, ring):
    across, right, left = [lax.ppermute(values, axis, step) for step in ring]
    return (values + across) + (right + left)


def sum_columns(values, beside=None):
    shape = values.shape
    flat = values.reshape(-1, shape[-1])
    if flat.size <= 32768:
        flat = flat + lax.ppermute(flat, "pcol", TWIN)
        return sum_ring(flat, "pcol", YRING).reshape(shape)
    halves = flat.reshape(2, -1, shape[-1])
    core = lax.axis_index("pcol") % 2
    mine = lax.dynamic_index_in_dim(halves, core, 0, keepdims=False)
    other = lax.dynamic_index_in_dim(halves, 1 - core, 0, keepdims=False)
    mine = mine + lax.ppermute(other, "pcol", TWIN)
    extra = None
    if beside is not None:
        mine, extra = beside(mine)
    mine = sum_ring(mine, "pcol", YRING)
    if beside is not None:
        mine, extra = lax.optimization_barrier((mine, extra))
    other = lax.ppermute(mine, "pcol", TWIN)
    both = jnp.where(core == 0, jnp.stack([mine, other]), jnp.stack([other, mine]))
    return both.reshape(shape) if beside is None else (both.reshape(shape), extra)


def sum_x_ring(values):
    shape = values.shape
    return sum_ring(values.reshape(-1, shape[-1]), "prow", XRING).reshape(shape)


def scatter_rows(values):
    chunks = values.reshape(ROWS, -1, values.shape[-1])
    return lax.all_to_all(chunks, "prow", 0, 0)


def share_rows(parts, shape):
    def kernel(parts, out):
        total = parts[0]
        for i in range(1, ROWS):
            total = total + parts[i]
        for i in range(ROWS):
            out[i] = total

    copies = call(kernel, [parts.shape], parts)[0]
    return lax.all_to_all(copies, "prow", 0, 0).reshape(shape)


def sum_rows(values):
    return share_rows(scatter_rows(values), values.shape)


def resident(array, *ranges):
    total = sum(len(blocks) for blocks in ranges)

    def kernel(source, *refs):
        arrived = refs[-1]
        copies = []
        for target, blocks in zip(refs, ranges):
            for i, block in enumerate(blocks):
                at = arrived.at[len(copies)]
                copies.append(pltpu.make_async_copy(source.at[block], target.at[i], at))
        for copy in copies:
            copy.start()
        for copy in copies:
            copy.wait()

    return pl.pallas_call(
        kernel,
        out_shape=[pltpu.VMEM((len(blocks),) + array.shape[1:], array.dtype) for blocks in ranges],
        in_specs=[pl.BlockSpec(memory_space=pltpu.HBM)],
        out_specs=[pl.BlockSpec(memory_space=pltpu.VMEM)] * len(ranges),
        scratch_shapes=[pltpu.SemaphoreType.DMA((total,))],
        compiler_params=grant(4),
    )(array)


def round_inverses(whole, count, at):
    def kernel(blocks, out):
        for i in range(count):
            for z in range(4):
                out[i, :, 128 * z : 128 * z + 128] = blocks[z, i].astype(jnp.bfloat16)

    return pl.pallas_call(
        kernel,
        out_shape=pltpu.VMEM((count, 256, 512), jnp.bfloat16),
        grid=(1,),
        in_specs=[pl.BlockSpec((4, count, 256, 128), lambda i: (0, at, 0, 0))],
        out_specs=pl.BlockSpec((count, 256, 512), lambda i: (0, 0, 0)),
        compiler_params=grant(12),
    )(whole)


def round_factors(whole, weights, count, at):
    def kernel(weights, blocks, out):
        for i in range(count):
            for z in range(4):
                for h in range(2):
                    values = blocks[z, i, 128 * h : 128 * h + 128, :] * weights[i]
                    rows = slice(128 * z, 128 * z + 128)
                    out[i, rows, 128 * h : 128 * h + 128] = values.astype(jnp.bfloat16)

    return pl.pallas_call(
        kernel,
        out_shape=pltpu.VMEM((count, 512, 256), jnp.bfloat16),
        grid=(1,),
        in_specs=[
            pl.BlockSpec(memory_space=pltpu.SMEM),
            pl.BlockSpec((4, count, 256, 128), lambda i: (0, at, 0, 0)),
        ],
        out_specs=pl.BlockSpec((count, 512, 256), lambda i: (0, 0, 0)),
        compiler_params=grant(12),
    )(weights, whole)


def gather_blocks(inverses, factors, after):
    halves = factors.reshape(-1, 128, 2, 128).transpose(0, 2, 1, 3).reshape(-1, 256, 128)
    own = jnp.concatenate([halves, inverses]).astype(jnp.float32)
    own, after = lax.optimization_barrier((own, after))
    whole = lax.all_gather(own, "prow", axis_index_groups=ZGROUPS)
    return whole, after


def call(kernel, shapes, *operands):
    outs = [pltpu.VMEM(shape, jnp.float32) for shape in shapes]
    return pl.pallas_call(kernel, out_shape=outs, compiler_params=grant(8))(*operands)


def dot(left, right, contract):
    dims = (((1,), (contract,)), ((), ()))
    return lax.dot_general(left, right, dims, preferred_element_type=jnp.float32)


def enter_split(order, total, inverses, sums_1, sums_0, here):
    def kernel(here, order, total, inverses, sums_1, sums_0, out):
        for n in range(4):
            rounded = (order[3 + n] - total[n]).astype(jnp.bfloat16)
            piece = dot(rounded, inverses[n], 1)
            for z in range(4):
                out[z, :, 256 * n : 256 * n + 256] = piece[16 * z : 16 * z + 16]
        for i, value in enumerate((sums_1[0], sums_1[1], sums_0[0])):
            value = value - order[(i + 1) % 3] * here[0]
            for z in range(4):
                out[z, :, 1024 + 128 * i : 1152 + 128 * i] = value[16 * z : 16 * z + 16]

    specs = [pl.BlockSpec(memory_space=pltpu.SMEM)] + [pl.BlockSpec(memory_space=pltpu.VMEM)] * 5
    return pl.pallas_call(
        kernel,
        out_shape=pltpu.VMEM((4, 16, 1408), jnp.float32),
        in_specs=specs,
        compiler_params=grant(8),
    )(here.reshape(1), order, total, inverses, sums_1, sums_0)


def entered_split(got):
    def kernel(got, pieces, sums_1, sums_0):
        for n in range(4):
            at = slice(256 * n, 256 * n + 256)
            pieces[n] = (got[0, :, at] + got[1, :, at]) + (got[2, :, at] + got[3, :, at])
        for i, out in enumerate((sums_1.at[0], sums_1.at[1], sums_0.at[0])):
            for z in range(4):
                out[:, 128 * z : 128 * z + 128] = got[z, :, 1024 + 128 * i : 1152 + 128 * i]

    return call(kernel, [(4, 16, 256), (2, 16, 512), (1, 16, 512)], got)


def leave_split(target, forward_2, forward_1, forward_0, solution_1, solution_0):
    def kernel(target, forward_2, forward_1, forward_0, solution_1, solution_0, out):
        lane = 0
        for part in (target, forward_2, forward_1, forward_0):
            for n in range(part.shape[0]):
                for z in range(4):
                    out[z, :, lane : lane + 256] = part[n]
                lane += 256
        for part in (solution_0, solution_1):
            for n in range(part.shape[0]):
                for z in range(4):
                    out[z, :, lane : lane + 128] = part[n, :, 128 * z : 128 * z + 128]
                lane += 128

    operands = (target, forward_2, forward_1, forward_0, solution_1, solution_0)
    return call(kernel, [(4, 16, 3200)], *operands)[0]


def left_split(got, inverses):
    def kernel(got, inverses, pieces, forward, solved):
        for n in range(4):
            rounded = got[:, 256 * n : 256 * n + 256].astype(jnp.bfloat16)
            pieces[n] = dot(rounded, inverses[n], 0)
            forward[3 + n] = got[:, 1024 + 256 * n : 1280 + 256 * n]
        for n in range(2):
            forward[1 + n] = got[:, 2048 + 256 * n : 2304 + 256 * n]
        forward[0] = got[:, 2560:2816]
        for n in range(3):
            solved[n] = got[:, 2816 + 128 * n : 2944 + 128 * n]

    shapes = [(4, 64, 128), (7, 64, 256), (3, 64, 128)]
    return call(kernel, shapes, got.reshape(64, 3200), inverses)


def per_device(rhs, factor, inverse, pattern):
    live = pattern.astype(jnp.float32)
    bf16 = jnp.bfloat16
    forward_levels = [None] * LEV
    far = (inverse, factor)
    partial_value = [[] for _ in range(LEV)]

    def push_up(narrow, tree_depth, first, last):
        for upward in range(first, last + 1):
            blocks = parent_at[tree_depth] if upward == 1 else blocks_of(factor, tree_depth, upward)
            terms = product(narrow, blocks, "nrc,nwc->nrw")
            terms = terms * blocks_of(live, tree_depth, upward)[:, None, None]
            partial_value[tree_depth - upward].append(sum_children(terms, upward))

    for tree_depth in range(LEV - 1, TOP - 1, -1):
        if tree_depth == LEV - 1:
            residual = nodes_of(rhs, tree_depth)
            blocks = nodes_of(inverse, tree_depth)
        else:
            residual = order[0] - sum_columns(sum(partial_value[tree_depth]))
            blocks = inverses[0]
        pieces = product(residual.astype(bf16), blocks, "nrc,nwc->nrw")
        if tree_depth == LEV - 1:
            near = lax.optimization_barrier((pieces, factor, inverse, rhs))
            pieces = near[0]
            parents = resident(near[1], range(34, 98, 4), range(10, 34, 3))
            inverses = resident(near[2], range(7, 15), range(3, 7))
            order = resident(near[3], range(7, 15))
        part = scatter_rows(pieces)
        if tree_depth == LEV - 1:
            part, parents, inverses, order = lax.optimization_barrier(
                (part, parents, inverses, order)
            )
            parent_at = {4: parents[0], 3: parents[1]}
            whole, part = gather_blocks(top_inverses(far[0]), top_order(far[1]), part)
        forward = share_rows(part, pieces.shape)
        forward_levels[tree_depth] = forward
        narrow = forward.astype(bf16)
        push_up(narrow, tree_depth, 1, tree_depth if tree_depth > TOP else 1)

    here = (lax.axis_index("pcol") == 0).astype(jnp.float32)
    total = sum(partial_value[2]).reshape(-1, 128)
    total = total + lax.ppermute(total, "pcol", TWIN)
    total, narrow = lax.optimization_barrier((total, narrow))
    total = sum_ring(total, "pcol", YRING).reshape(4, 64, 128)
    push_up(narrow, TOP, 2, TOP)
    sent = enter_split(
        rhs[0:7], total, inverses[1], sum(partial_value[1]), sum(partial_value[0]), here
    )
    got = lax.all_to_all(sent, "prow", 0, 0, axis_index_groups=ZGROUPS)
    pieces, sums_1, sums_0 = entered_split(got)
    pieces, whole = lax.optimization_barrier((pieces, whole))
    weights = top_order(live)
    parents = round_factors(whole, weights[0:4], 4, 0)
    roots = round_factors(whole, weights[4:8], 4, 1)
    children = round_factors(whole, weights[8:10], 2, 4)
    inverse_at = [round_inverses(whole, 1, 12), round_inverses(whole, 2, 5)]
    top_forward = [None] * TOP
    top_forward[2] = sum_x_ring(pieces)
    top_partial = [[sums_0], [sums_1]]

    def split_up(narrow, tree_depth):
        for upward in range(1, tree_depth + 1):
            terms = product(narrow, factor_at[tree_depth][upward - 1], "nrc,nwc->nrw")
            top_partial[tree_depth - upward].append(sum_children(terms, upward))

    factor_at = [None, [children], [parents, roots]]
    split_up(top_forward[2].astype(bf16), 2)
    for tree_depth in (1, 0):
        residual = -sum_columns(sum(top_partial[tree_depth]))
        pieces = product(residual.astype(bf16), inverse_at[tree_depth], "nrc,nwc->nrw")
        top_forward[tree_depth] = sum_x_ring(pieces)
        if tree_depth:
            split_up(top_forward[1].astype(bf16), 1)

    top_solved = []
    for tree_depth in range(TOP):
        target = top_forward[tree_depth]
        if tree_depth:
            terms = 0.0
            for upward in range(tree_depth, 0, -1):
                above = jnp.repeat(
                    top_solved[tree_depth - upward].astype(bf16), 2**upward, axis=0
                )
                blocks = factor_at[tree_depth][upward - 1]
                terms = terms + product(above, blocks, "nrw,nwc->nrc")
            target = target - sum_x_ring(terms)
        if tree_depth < TOP - 1:
            pieces = product(target.astype(bf16), inverse_at[tree_depth], "nrw,nwc->nrc")
            top_solved.append(sum_columns(pieces))

    sent = leave_split(target, *top_forward[::-1], top_solved[1], top_solved[0])
    got = lax.all_to_all(sent, "prow", 0, 0, axis_index_groups=ZGROUPS)
    pieces, top_forward, top_solved = left_split(got, inverses[1])

    gathered = [[] for _ in range(LEV)]

    def push_down(narrow, tree_depth):
        for lower in range(max(tree_depth + 1, TOP), LEV):
            upward = lower - tree_depth
            above = jnp.repeat(narrow, 2**upward, axis=0)
            blocks = parent_at[lower] if upward == 1 else blocks_of(factor, lower, upward)
            terms = product(above, blocks, "nrw,nwc->nrc")
            gathered[lower].append(terms * blocks_of(live, lower, upward)[:, None, None])

    for tree_depth in (0, 1):
        push_down(nodes_of(top_solved, tree_depth).astype(bf16), tree_depth)
    solved = [top_solved]
    for tree_depth in range(TOP - 1, LEV):
        if tree_depth >= TOP:
            target = forward_levels[tree_depth] - sum_rows(sum(gathered[tree_depth]))
            blocks = inverses[0] if tree_depth == TOP else nodes_of(inverse, tree_depth)
            pieces = product(target.astype(bf16), blocks, "nrw,nwc->nrc")
        if tree_depth < LEV - 1:
            solution = sum_columns(pieces)
            solved.append(solution)
            push_down(solution.astype(bf16), tree_depth)

    def outputs(mine):
        levels = [top_forward] + forward_levels[TOP:]
        mine, upper, levels = lax.optimization_barrier((mine, solved, levels))
        whole = jnp.zeros(rhs.shape, jnp.float32).at[:15].set(jnp.concatenate(upper))
        return mine, (whole, jnp.concatenate(levels))

    solution, (upper, forward_whole) = sum_columns(pieces, outputs)
    return upper.at[15:].set(solution), forward_whole


def solution(mesh):
    in_specs = (P(None, None, "prow"), P(None, "prow", "pcol"), P(None, "pcol", "prow"), P())
    out_specs = (P(None, None, "prow"), P(None, None, "pcol"))
    return jax.shard_map(
        per_device, mesh=mesh, in_specs=in_specs, out_specs=out_specs, check_vma=False
    )
```

```python
import jax
import jax.numpy as jnp
from jax import lax
from jax.experimental import pallas as pl
from jax.experimental.pallas import tpu as pltpu
from jax.sharding import PartitionSpec as P

LEV = 5
ROWS = 16
TOP = 3
TWIN = [(i, i ^ 1) for i in range(8)]
YRING = [[(i, (i + 2 * k) % 8) for i in range(8)] for k in (2, 1, 3)]
XRING = [[(i, (i + 4 * k) % 16) for i in range(16)] for k in (2, 1, 3)]
ZGROUPS = [[4 * x + z for z in range(4)] for x in range(4)]


def block_start(tree_depth):
    return (tree_depth - 2) * 2**tree_depth + 2


def blocks_of(array, tree_depth, upward):
    start = block_start(tree_depth)
    count = 2**tree_depth
    return array[start + upward - 1 : start + count * tree_depth : tree_depth]


def nodes_of(array, tree_depth):
    return array[2**tree_depth - 1 : 2 ** (tree_depth + 1) - 1]


def product(left, right, form):
    return jnp.einsum(form, left, right, preferred_element_type=jnp.float32)


def grant(megabytes):
    return pltpu.CompilerParams(vmem_limit_bytes=megabytes << 20)


def sum_children(terms, upward):
    return terms.reshape((-1, 2**upward) + terms.shape[1:]).sum(axis=1)


def top_order(array):
    return jnp.concatenate([array[2:10:2], array[3:10:2], array[0:2]])


def top_inverses(array):
    return jnp.concatenate([array[1:3], array[0:1]])


def sum_ring(values, axis, ring):
    across, right, left = [lax.ppermute(values, axis, step) for step in ring]
    return (values + across) + (right + left)


def sum_columns(values, beside=None):
    shape = values.shape
    flat = values.reshape(-1, shape[-1])
    if flat.size <= 32768:
        flat = flat + lax.ppermute(flat, "pcol", TWIN)
        return sum_ring(flat, "pcol", YRING).reshape(shape)
    halves = flat.reshape(2, -1, shape[-1])
    core = lax.axis_index("pcol") % 2
    mine = lax.dynamic_index_in_dim(halves, core, 0, keepdims=False)
    other = lax.dynamic_index_in_dim(halves, 1 - core, 0, keepdims=False)
    mine = mine + lax.ppermute(other, "pcol", TWIN)
    extra = None
    if beside is not None:
        mine, extra = beside(mine)
    mine = sum_ring(mine, "pcol", YRING)
    if beside is not None:
        mine, extra = lax.optimization_barrier((mine, extra))
    other = lax.ppermute(mine, "pcol", TWIN)
    both = jnp.where(core == 0, jnp.stack([mine, other]), jnp.stack([other, mine]))
    return both.reshape(shape) if beside is None else (both.reshape(shape), extra)


def sum_x_ring(values):
    shape = values.shape
    return sum_ring(values.reshape(-1, shape[-1]), "prow", XRING).reshape(shape)


def scatter_rows(values):
    chunks = values.reshape(ROWS, -1, values.shape[-1])
    return lax.all_to_all(chunks, "prow", 0, 0)


def share_rows(parts, shape):
    def kernel(parts, out):
        total = parts[0]
        for i in range(1, ROWS):
            total = total + parts[i]
        for i in range(ROWS):
            out[i] = total

    copies = call(kernel, [parts.shape], parts)[0]
    return lax.all_to_all(copies, "prow", 0, 0).reshape(shape)


def sum_rows(values):
    return share_rows(scatter_rows(values), values.shape)


def resident(array, *ranges):
    total = sum(len(blocks) for blocks in ranges)

    def kernel(source, *refs):
        arrived = refs[-1]
        copies = []
        for target, blocks in zip(refs, ranges):
            for i, block in enumerate(blocks):
                at = arrived.at[len(copies)]
                copies.append(pltpu.make_async_copy(source.at[block], target.at[i], at))
        for copy in copies:
            copy.start()
        for copy in copies:
            copy.wait()

    return pl.pallas_call(
        kernel,
        out_shape=[pltpu.VMEM((len(blocks),) + array.shape[1:], array.dtype) for blocks in ranges],
        in_specs=[pl.BlockSpec(memory_space=pltpu.HBM)],
        out_specs=[pl.BlockSpec(memory_space=pltpu.VMEM)] * len(ranges),
        scratch_shapes=[pltpu.SemaphoreType.DMA((total,))],
        compiler_params=grant(4),
    )(array)


def round_inverses(whole, count, at):
    def kernel(blocks, out):
        for i in range(count):
            for z in range(4):
                out[i, :, 128 * z : 128 * z + 128] = blocks[z, i].astype(jnp.bfloat16)

    return pl.pallas_call(
        kernel,
        out_shape=pltpu.VMEM((count, 256, 512), jnp.bfloat16),
        grid=(1,),
        in_specs=[pl.BlockSpec((4, count, 256, 128), lambda i: (0, at, 0, 0))],
        out_specs=pl.BlockSpec((count, 256, 512), lambda i: (0, 0, 0)),
        compiler_params=grant(12),
    )(whole)


def round_factors(whole, weights, count, at):
    def kernel(weights, blocks, out):
        for i in range(count):
            for z in range(4):
                for h in range(2):
                    values = blocks[z, i, 128 * h : 128 * h + 128, :] * weights[i]
                    rows = slice(128 * z, 128 * z + 128)
                    out[i, rows, 128 * h : 128 * h + 128] = values.astype(jnp.bfloat16)

    return pl.pallas_call(
        kernel,
        out_shape=pltpu.VMEM((count, 512, 256), jnp.bfloat16),
        grid=(1,),
        in_specs=[
            pl.BlockSpec(memory_space=pltpu.SMEM),
            pl.BlockSpec((4, count, 256, 128), lambda i: (0, at, 0, 0)),
        ],
        out_specs=pl.BlockSpec((count, 512, 256), lambda i: (0, 0, 0)),
        compiler_params=grant(12),
    )(weights, whole)


def gather_blocks(inverses, factors, after):
    halves = factors.reshape(-1, 128, 2, 128).transpose(0, 2, 1, 3).reshape(-1, 256, 128)
    own = jnp.concatenate([halves, inverses]).astype(jnp.float32)
    own, after = lax.optimization_barrier((own, after))
    whole = lax.all_gather(own, "prow", axis_index_groups=ZGROUPS)
    return whole, after


def call(kernel, shapes, *operands):
    outs = [pltpu.VMEM(shape, jnp.float32) for shape in shapes]
    return pl.pallas_call(kernel, out_shape=outs, compiler_params=grant(8))(*operands)


def dot(left, right, contract):
    dims = (((1,), (contract,)), ((), ()))
    return lax.dot_general(left, right, dims, preferred_element_type=jnp.float32)


def enter_split(order, total, inverses, sums_1, sums_0, here):
    def kernel(here, order, total, inverses, sums_1, sums_0, out):
        for n in range(4):
            rounded = (order[3 + n] - total[n]).astype(jnp.bfloat16)
            piece = dot(rounded, inverses[n], 1)
            for z in range(4):
                out[z, :, 256 * n : 256 * n + 256] = piece[16 * z : 16 * z + 16]
        for i, value in enumerate((sums_1[0], sums_1[1], sums_0[0])):
            value = value - order[(i + 1) % 3] * here[0]
            for z in range(4):
                out[z, :, 1024 + 128 * i : 1152 + 128 * i] = value[16 * z : 16 * z + 16]

    specs = [pl.BlockSpec(memory_space=pltpu.SMEM)] + [pl.BlockSpec(memory_space=pltpu.VMEM)] * 5
    return pl.pallas_call(
        kernel,
        out_shape=pltpu.VMEM((4, 16, 1408), jnp.float32),
        in_specs=specs,
        compiler_params=grant(8),
    )(here.reshape(1), order, total, inverses, sums_1, sums_0)


def entered_split(got):
    def kernel(got, pieces, sums_1, sums_0):
        for n in range(4):
            at = slice(256 * n, 256 * n + 256)
            pieces[n] = (got[0, :, at] + got[1, :, at]) + (got[2, :, at] + got[3, :, at])
        for i, out in enumerate((sums_1.at[0], sums_1.at[1], sums_0.at[0])):
            for z in range(4):
                out[:, 128 * z : 128 * z + 128] = got[z, :, 1024 + 128 * i : 1152 + 128 * i]

    return call(kernel, [(4, 16, 256), (2, 16, 512), (1, 16, 512)], got)


def leave_split(target, forward_2, forward_1, forward_0, solution_1, solution_0):
    def kernel(target, forward_2, forward_1, forward_0, solution_1, solution_0, out):
        lane = 0
        for part in (target, forward_2, forward_1, forward_0):
            for n in range(part.shape[0]):
                for z in range(4):
                    out[z, :, lane : lane + 256] = part[n]
                lane += 256
        for part in (solution_0, solution_1):
            for n in range(part.shape[0]):
                for z in range(4):
                    out[z, :, lane : lane + 128] = part[n, :, 128 * z : 128 * z + 128]
                lane += 128

    operands = (target, forward_2, forward_1, forward_0, solution_1, solution_0)
    return call(kernel, [(4, 16, 3200)], *operands)[0]


def left_split(got, inverses):
    def kernel(got, inverses, pieces, forward, solved):
        for n in range(4):
            rounded = got[:, 256 * n : 256 * n + 256].astype(jnp.bfloat16)
            pieces[n] = dot(rounded, inverses[n], 0)
            forward[3 + n] = got[:, 1024 + 256 * n : 1280 + 256 * n]
        for n in range(2):
            forward[1 + n] = got[:, 2048 + 256 * n : 2304 + 256 * n]
        forward[0] = got[:, 2560:2816]
        for n in range(3):
            solved[n] = got[:, 2816 + 128 * n : 2944 + 128 * n]

    shapes = [(4, 64, 128), (7, 64, 256), (3, 64, 128)]
    return call(kernel, shapes, got.reshape(64, 3200), inverses)


def per_device(rhs, factor, inverse, pattern):
    live = pattern.astype(jnp.float32)
    bf16 = jnp.bfloat16
    forward_levels = [None] * LEV
    far = (inverse, factor)
    partial_value = [[] for _ in range(LEV)]

    def push_up(narrow, tree_depth, first, last):
        for upward in range(first, last + 1):
            blocks = parent_at[tree_depth] if upward == 1 else blocks_of(factor, tree_depth, upward)
            terms = product(narrow, blocks, "nrc,nwc->nrw")
            terms = terms * blocks_of(live, tree_depth, upward)[:, None, None]
            partial_value[tree_depth - upward].append(sum_children(terms, upward))

    for tree_depth in range(LEV - 1, TOP - 1, -1):
        if tree_depth == LEV - 1:
            residual = nodes_of(rhs, tree_depth)
            blocks = nodes_of(inverse, tree_depth)
        else:
            residual = order[0] - sum_columns(sum(partial_value[tree_depth]))
            blocks = inverses[0]
        pieces = product(residual.astype(bf16), blocks, "nrc,nwc->nrw")
        if tree_depth == LEV - 1:
            near = lax.optimization_barrier((pieces, factor, inverse, rhs))
            pieces = near[0]
            parents = resident(near[1], range(34, 98, 4), range(10, 34, 3))
            inverses = resident(near[2], range(7, 15), range(3, 7), range(15, 31))
            order = resident(near[3], range(7, 15))
        part = scatter_rows(pieces)
        if tree_depth == LEV - 1:
            part, parents, inverses, order = lax.optimization_barrier(
                (part, parents, inverses, order)
            )
            parent_at = {4: parents[0], 3: parents[1]}
            whole, part = gather_blocks(top_inverses(far[0]), top_order(far[1]), part)
        forward = share_rows(part, pieces.shape)
        forward_levels[tree_depth] = forward
        narrow = forward.astype(bf16)
        push_up(narrow, tree_depth, 1, tree_depth if tree_depth > TOP else 1)

    here = (lax.axis_index("pcol") == 0).astype(jnp.float32)
    total = sum(partial_value[2]).reshape(-1, 128)
    total = total + lax.ppermute(total, "pcol", TWIN)
    total, narrow = lax.optimization_barrier((total, narrow))
    total = sum_ring(total, "pcol", YRING).reshape(4, 64, 128)
    push_up(narrow, TOP, 2, TOP)
    sent = enter_split(
        rhs[0:7], total, inverses[1], sum(partial_value[1]), sum(partial_value[0]), here
    )
    got = lax.all_to_all(sent, "prow", 0, 0, axis_index_groups=ZGROUPS)
    pieces, sums_1, sums_0 = entered_split(got)
    pieces, whole = lax.optimization_barrier((pieces, whole))
    weights = top_order(live)
    parents = round_factors(whole, weights[0:4], 4, 0)
    roots = round_factors(whole, weights[4:8], 4, 1)
    children = round_factors(whole, weights[8:10], 2, 4)
    inverse_at = [round_inverses(whole, 1, 12), round_inverses(whole, 2, 5)]
    top_forward = [None] * TOP
    top_forward[2] = sum_x_ring(pieces)
    top_partial = [[sums_0], [sums_1]]

    def split_up(narrow, tree_depth):
        for upward in range(1, tree_depth + 1):
            terms = product(narrow, factor_at[tree_depth][upward - 1], "nrc,nwc->nrw")
            top_partial[tree_depth - upward].append(sum_children(terms, upward))

    factor_at = [None, [children], [parents, roots]]
    split_up(top_forward[2].astype(bf16), 2)
    for tree_depth in (1, 0):
        residual = -sum_columns(sum(top_partial[tree_depth]))
        pieces = product(residual.astype(bf16), inverse_at[tree_depth], "nrc,nwc->nrw")
        top_forward[tree_depth] = sum_x_ring(pieces)
        if tree_depth:
            split_up(top_forward[1].astype(bf16), 1)

    top_solved = []
    for tree_depth in range(TOP):
        target = top_forward[tree_depth]
        if tree_depth:
            terms = 0.0
            for upward in range(tree_depth, 0, -1):
                above = jnp.repeat(
                    top_solved[tree_depth - upward].astype(bf16), 2**upward, axis=0
                )
                blocks = factor_at[tree_depth][upward - 1]
                terms = terms + product(above, blocks, "nrw,nwc->nrc")
            target = target - sum_x_ring(terms)
        if tree_depth < TOP - 1:
            pieces = product(target.astype(bf16), inverse_at[tree_depth], "nrw,nwc->nrc")
            top_solved.append(sum_columns(pieces))

    sent = leave_split(target, *top_forward[::-1], top_solved[1], top_solved[0])
    got = lax.all_to_all(sent, "prow", 0, 0, axis_index_groups=ZGROUPS)
    pieces, top_forward, top_solved = left_split(got, inverses[1])

    gathered = [[] for _ in range(LEV)]

    def push_down(narrow, tree_depth):
        for lower in range(max(tree_depth + 1, TOP), LEV):
            upward = lower - tree_depth
            above = jnp.repeat(narrow, 2**upward, axis=0)
            blocks = parent_at[lower] if upward == 1 else blocks_of(factor, lower, upward)
            terms = product(above, blocks, "nrw,nwc->nrc")
            gathered[lower].append(terms * blocks_of(live, lower, upward)[:, None, None])

    for tree_depth in (0, 1):
        push_down(nodes_of(top_solved, tree_depth).astype(bf16), tree_depth)
    solved = [top_solved]
    for tree_depth in range(TOP - 1, LEV):
        if tree_depth >= TOP:
            target = forward_levels[tree_depth] - sum_rows(sum(gathered[tree_depth]))
            blocks = inverses[0] if tree_depth == TOP else inverses[2]
            pieces = product(target.astype(bf16), blocks, "nrw,nwc->nrc")
        if tree_depth < LEV - 1:
            solution = sum_columns(pieces)
            solved.append(solution)
            push_down(solution.astype(bf16), tree_depth)

    def outputs(mine):
        levels = [top_forward] + forward_levels[TOP:]
        mine, upper, levels = lax.optimization_barrier((mine, solved, levels))
        whole = jnp.zeros(rhs.shape, jnp.float32).at[:15].set(jnp.concatenate(upper))
        return mine, (whole, jnp.concatenate(levels))

    solution, (upper, forward_whole) = sum_columns(pieces, outputs)
    return upper.at[15:].set(solution), forward_whole


def solution(mesh):
    in_specs = (P(None, None, "prow"), P(None, "prow", "pcol"), P(None, "pcol", "prow"), P())
    out_specs = (P(None, None, "prow"), P(None, None, "pcol"))
    return jax.shard_map(
        per_device, mesh=mesh, in_specs=in_specs, out_specs=out_specs, check_vma=False
    )
```
